32 devices in a mesh: dp: 16 (over z, y, x), expert: 2 (over core).
Axes of the slice: x: 2, y: 2, z: 4, core: 2. Of those that a mesh axis runs over, the one named last changes fastest.
Arguments:
- latents: bfloat16 [4096, 2048], P('dp', 'expert'), as said below
- cotangent: bfloat16 [4096, 2048], P('dp', 'expert'), may hold values from -6 to 6
- routes: int32 [4096, 2], P('dp'), may hold values from 0 to 15, all different within a row; in each aligned block of 256 rows (0 to 255, 256 to 511, ...) at most 48 rows name the same one
- router_w: float32 [2048, 16], P('expert'), may hold values from -1 to 1
- mod_shift: bfloat16 [1, 2048], P(None, 'expert'), may hold values from -3 to 3
- mod_scale: bfloat16 [1, 2048], P(None, 'expert'), may hold values from -1.5 to 2.5
- mod_gate: bfloat16 [1, 2048], P(None, 'expert'), may hold values from -4 to 4
- gate_w: bfloat16 [16, 2048, 1024], P('dp', None, 'expert'), may hold values from -0.125 to 0.125
- up_w: bfloat16 [16, 2048, 1024], P('dp', None, 'expert'), may hold values from -0.125 to 0.125
- down_w: bfloat16 [16, 1024, 2048], P('dp', 'expert'), may hold values from -0.1875 to 0.1875
Outputs:
- latent_gradient: bfloat16 [4096, 2048], P('dp', 'expert')
- grad_gate_w: bfloat16 [16, 2048, 1024], P('dp', None, 'expert')
- grad_up_w: bfloat16 [16, 2048, 1024], P('dp', None, 'expert')
- grad_down_w: bfloat16 [16, 1024, 2048], P('dp', 'expert')
- grad_router: float32 [2048, 16], P('expert')
The draws below stay inside these ranges and needn't reach their ends.
Inputs may be any that keep to these rules, and one draw needn't show every extreme that they name: `routes`: the two experts of a token differ. Among the 256 tokens of one aligned block (the tokens of one index of dp), no expert is named more than 48 times, a bound that some block reaches. Columns and rows of latents have unlike scales.
All inputs are finite; a program needn't handle non-finite values.
Results may differ from the reference program's by a relative error of at most 0.008.
Values may be sent and summed in bfloat16 or wider, within the bound.
No kernel may reach another device: no remote copies, remote signals or barrier semaphores. Data moves between devices by JAX's collectives and lax.ppermute only.
A program may use at most 128 MiB of HBM per device.

```python
import math
import jax
import jax.numpy as jnp
import numpy as np
from jax import lax

D = 2048
HID = 1024
SEQ = 4096
TOK_DEV = 256
EXPERTS = 16
TOKENS = 4096
SAMPLES = 1
CAP = 48
N_DP = 16
N_EXPERT = 2


def draw_latents(key, part):
    key_base, key_cols, key_rows = jax.random.split(key, 3)
    column_pos = jnp.arange(D, dtype=jnp.float32) / max(D - 1, 1)
    trend = jnp.exp(math.log(3.0) * column_pos)
    spread = jnp.exp(jax.random.uniform(key_cols, (D,), jnp.float32, 0.0, math.log(10.0)))
    row_scale = jnp.exp(jax.random.uniform(key_rows, (TOKENS, 1), jnp.float32, math.log(0.7), math.log(1.4)))
    base = jax.random.normal(key_base, (TOKENS, D), jnp.float32)
    return (0.25 * base * row_scale * trend * spread).astype(jnp.bfloat16)


def draw_cotangent(key, part):
    key_base = jax.random.fold_in(key, 31)
    base = jnp.clip(jax.random.normal(key_base, (TOKENS, D), jnp.float32), -6.0, 6.0)
    return base.astype(jnp.bfloat16)


def draw_mod_gate(key, part):
    key_base = jax.random.fold_in(key, 37)
    base = jnp.clip(jax.random.normal(key_base, (SAMPLES, D), jnp.float32), -4.0, 4.0)
    return base.astype(jnp.bfloat16)


def draw_router_w(key, part):
    key_base, key_sign = jax.random.split(jax.random.fold_in(key, 11), 2)
    base = jnp.clip(jax.random.normal(key_base, (D, EXPERTS), jnp.float32), -5.0, 5.0)
    offset_size = 0.01
    offset = jnp.where(jax.random.uniform(key_sign, (1, EXPERTS), jnp.float32) < 0.5, -offset_size, offset_size)
    return 0.5 * base * D ** (-0.5) + offset


def draw_mod_scale(key, part):
    key_noise = jax.random.fold_in(key, 23)
    column_pos = jnp.arange(D, dtype=jnp.float32) / max(D - 1, 1)
    ramp = -0.5 + 1.5 * column_pos
    noise = 0.15 * jnp.clip(jax.random.normal(key_noise, (SAMPLES, D), jnp.float32), -3.0, 3.0)
    return (ramp[None, :] + noise).astype(jnp.bfloat16)


def levels(stream_key, extent, cuts, least, top_value):
    def one(dim, shards_of):
        heights = jax.random.uniform(jax.random.fold_in(jax.random.fold_in(stream_key, 6), dim), (shards_of,), jnp.float32, least / len(cuts), top_value / len(cuts))
        return jnp.repeat(jnp.exp(heights), extent[dim] // shards_of).reshape((-1,) + (1,) * (len(extent) - dim - 1))

    loudness = one(*cuts[0])
    for cut in cuts[1:]:
        loudness = loudness * one(*cut)
    return loudness


def deal_out(stream_key, own, number, rows, number_of, top, reach, skew):
    order = jax.random.permutation(stream_key, number_of)
    heavy_load, ordinary = shares(number_of, rows * top, reach, skew, True), shares(number_of, rows * top, reach, skew, False)
    places = jnp.arange(number_of)

    def named(sizes, offset_by):
        used = int((sizes > 0).sum())
        fixed = max(1, used // 4)
        shifted = fixed + (places - fixed + offset_by * (used - fixed)) % max(1, number_of - fixed)
        return jnp.zeros((number_of,), jnp.int32).at[order[jnp.where(places < fixed, places, shifted)]].set(jnp.asarray(sizes, jnp.int32))

    sizes = jnp.where(number % 4 == 0, named(heavy_load, number // 4), named(ordinary, number - number // 4 - 1))
    mixed = jax.random.permutation(jax.random.fold_in(own, 3), number_of)
    source_of, receiver = mixed[0:number_of // 2 * 2:2], mixed[1:number_of // 2 * 2:2]
    margin = jnp.minimum(sizes[source_of] - 1, reach - sizes[receiver]) // 2
    margin = jnp.where((source_of == order[0]) | (receiver == order[0]) | (sizes[receiver] == 0), 0, jnp.maximum(margin, 0))
    shifted = jax.random.randint(jax.random.fold_in(own, 4), (number_of // 2,), 0, 1 << 20) % (margin + 1)
    sizes = sizes.at[source_of].add(-shifted).at[receiver].add(shifted)
    members = jnp.searchsorted(jnp.cumsum(sizes), jnp.arange(rows * top), side="right").astype(jnp.int32)
    listing = members.reshape(top, rows).T
    listing = listing[jax.random.permutation(jax.random.fold_in(own, 1), rows)]
    offset_by = jax.random.randint(jax.random.fold_in(own, 2), (rows, 1), 0, top)
    return jnp.take_along_axis(listing, (jnp.arange(top)[None, :] + offset_by) % top, axis=1)


def shares(count, total, limit, skew, full):
    portions = [(1 << 20) // math.isqrt(rank ** skew) + 1 for rank in range(1, count + 1)]
    largest = limit if full else min(limit, max(-(-total // count), total * portions[0] // sum(portions)))
    least = 1 if total - largest >= count - 1 else 0
    counts, rest = [largest] + [least] * (count - 1), total - largest - least * (count - 1)
    while rest > 0:
        free = [i for i in range(1, count) if counts[i] < largest] or [i for i in range(1, count) if counts[i] < limit]
        mass, budget = sum([portions[i] for i in free]), rest
        for i in free:
            more = min(limit - counts[i], max(1, budget * portions[i] // mass), rest)
            counts[i] = counts[i] + more
            rest = rest - more
    return np.array(counts)


def gaussian(own_key, dims, width, bound, shards=(), kind=jnp.bfloat16):
    level = levels(own_key, dims, shards, -0.22, 0.18) if shards else 1.0
    values = jax.random.normal(own_key, dims, jnp.float32) * width * level
    return jnp.minimum(jnp.maximum(values, -bound), bound).astype(kind)


def setup_inputs(seed: int = 0) -> dict:
    streams_of = jax.random.split(jax.random.key(seed), 11)
    latents = draw_latents(jax.random.fold_in(streams_of[10], 71), 0)
    cotangent = draw_cotangent(jax.random.fold_in(streams_of[10], 71), 0)
    routes_keys = jax.random.split(jax.random.fold_in(streams_of[2], 1), TOKENS // TOK_DEV)
    routes_turns = jax.random.permutation(jax.random.fold_in(streams_of[2], 3), TOKENS // TOK_DEV)
    routes = jax.vmap(lambda own, number: deal_out(jax.random.fold_in(streams_of[2], 2), own, number, TOK_DEV, EXPERTS, 2, CAP, 2))(routes_keys, routes_turns).reshape((TOKENS, 2))
    router_w = draw_router_w(jax.random.fold_in(streams_of[10], 71), 0)
    mod_shift = gaussian(streams_of[4], (SAMPLES, D), 0.5, 3.0, ((1, 2),))
    mod_scale = draw_mod_scale(jax.random.fold_in(streams_of[10], 71), 0)
    mod_gate = draw_mod_gate(jax.random.fold_in(streams_of[10], 71), 0)
    gate_w = gaussian(streams_of[7], (EXPERTS, D, HID), D ** -0.5, 0.125, ((0, 16), (2, 2)))
    up_w = gaussian(streams_of[8], (EXPERTS, D, HID), D ** -0.5, 0.125, ((0, 16), (2, 2)))
    down_w = gaussian(streams_of[9], (EXPERTS, HID, D), HID ** -0.5, 0.1875, ((0, 16), (1, 2)))
    return dict(latents=latents, cotangent=cotangent, routes=routes, router_w=router_w, mod_shift=mod_shift, mod_scale=mod_scale, mod_gate=mod_gate, gate_w=gate_w, up_w=up_w, down_w=down_w)


norm_eps = 1e-06

def reference(latents, cotangent, routes, router_w, mod_shift, mod_scale, mod_gate, gate_w, up_w, down_w):
    highest = lax.Precision.HIGHEST
    latent_rows_f32 = latents.astype(jnp.float32)
    output_gradient_f32 = cotangent.astype(jnp.float32)
    row_average = lax.optimization_barrier(jnp.mean(latent_rows_f32, axis=1, keepdims=True))
    row_msq = lax.optimization_barrier(jnp.mean(latent_rows_f32 * latent_rows_f32, axis=1, keepdims=True))
    inverse_deviation = lax.rsqrt(row_msq - row_average * row_average + norm_eps)
    centered_scaled = (latent_rows_f32 - row_average) * inverse_deviation
    modulation_amplitude = 1.0 + jnp.repeat(mod_scale.astype(jnp.float32), SEQ, axis=0)
    shift_row_values = jnp.repeat(mod_shift.astype(jnp.float32), SEQ, axis=0)
    gate_rows = jnp.repeat(mod_gate.astype(jnp.float32), SEQ, axis=0)
    normed_rows = centered_scaled * modulation_amplitude + shift_row_values
    normed_b = normed_rows.astype(jnp.bfloat16)
    logits = jnp.dot(normed_rows, router_w, precision=highest)
    chances = jax.nn.sigmoid(logits)
    expert_ids = jnp.arange(EXPERTS, dtype=jnp.int32)
    hits = routes[:, :, None] == expert_ids[None, None, :]
    picked = lax.optimization_barrier(jnp.sum(jnp.where(hits, chances[:, None, :], 0.0), axis=2))
    pick_sum = lax.optimization_barrier(jnp.sum(picked, axis=1, keepdims=True))
    weights = picked / pick_sum
    weights_b = weights.astype(jnp.bfloat16)
    scaled_dy = (gate_rows * output_gradient_f32).astype(jnp.bfloat16)
    flat_routes = routes.reshape(N_DP, TOK_DEV * 2)
    onehot = (flat_routes[:, :, None] == expert_ids[None, None, :]).astype(jnp.int32)
    rank_run = jnp.cumsum(onehot, axis=1) - 1
    slot_pos = lax.optimization_barrier(jnp.sum(onehot * rank_run, axis=2))
    row_pos = jnp.arange(N_DP, dtype=jnp.int32)[:, None] * CAP + slot_pos
    assign_ids = jnp.arange(TOKENS * 2, dtype=jnp.int32).reshape(N_DP, TOK_DEV * 2)
    table = jnp.full((EXPERTS, N_DP * CAP), -1, jnp.int32)
    table = table.at[flat_routes.reshape(-1), row_pos.reshape(-1)].set(assign_ids.reshape(-1))
    flat_w = weights.reshape(-1)
    flat_wb = weights_b.reshape(-1)
    block_width = HID // N_EXPERT

    def per_expert(totals, inputs):
        combined, scores = totals
        index_row, wgate, wup, wdown = inputs
        valid = index_row >= 0
        safe_ids = jnp.maximum(index_row, 0)
        token_ids = safe_ids // 2
        rows_x = jnp.where(valid[:, None], normed_b[token_ids], jnp.zeros((), jnp.bfloat16)).astype(jnp.bfloat16)
        rows_z = jnp.where(valid[:, None], scaled_dy[token_ids], jnp.zeros((), jnp.bfloat16)).astype(jnp.bfloat16)
        slot_w = jnp.where(valid, flat_wb[safe_ids].astype(jnp.float32), 0.0)
        gate_lin = jnp.dot(rows_x, wgate, preferred_element_type=jnp.float32)
        up_lin = jnp.dot(rows_x, wup, preferred_element_type=jnp.float32)
        down_back = jnp.dot(rows_z, wdown.T, preferred_element_type=jnp.float32)
        gate_sig = jax.nn.sigmoid(gate_lin)
        gate_act = gate_lin * gate_sig
        hidden = gate_act * up_lin
        slot_score = lax.optimization_barrier(jnp.sum(hidden * down_back, axis=1))
        d_gate = down_back * up_lin * gate_sig * (1.0 + gate_lin * (1.0 - gate_sig))
        d_up = down_back * gate_act
        d_gate_b = d_gate.astype(jnp.bfloat16)
        d_up_b = d_up.astype(jnp.bfloat16)
        returned = jnp.zeros((N_DP * CAP, D), jnp.float32)
        for block in range(N_EXPERT):
            low = block * block_width
            high = low + block_width
            term = jnp.dot(d_gate_b[:, low:high], wgate[:, low:high].T, preferred_element_type=jnp.float32)
            term = term + jnp.dot(d_up_b[:, low:high], wup[:, low:high].T, preferred_element_type=jnp.float32)
            term = lax.optimization_barrier(term.astype(jnp.bfloat16)).astype(jnp.float32)
            returned = returned + term
        scale_col = slot_w[:, None]
        gate_wt = (scale_col * d_gate).astype(jnp.bfloat16)
        up_wt = (scale_col * d_up).astype(jnp.bfloat16)
        hidden_wt = (scale_col * hidden).astype(jnp.bfloat16)
        grad_gate = jnp.dot(rows_x.T, gate_wt, preferred_element_type=jnp.float32).astype(jnp.bfloat16)
        grad_up = jnp.dot(rows_x.T, up_wt, preferred_element_type=jnp.float32).astype(jnp.bfloat16)
        grad_down = jnp.dot(hidden_wt.T, rows_z, preferred_element_type=jnp.float32).astype(jnp.bfloat16)
        token_w = jnp.where(valid, flat_w[safe_ids], 0.0)
        combined = combined.at[token_ids].add(token_w[:, None] * returned)
        scores = scores.at[safe_ids].add(jnp.where(valid, slot_score, 0.0))
        return ((combined, scores), (grad_gate, grad_up, grad_down))
    start_totals = (jnp.zeros((TOKENS, D), jnp.float32), jnp.zeros((TOKENS * 2,), jnp.float32))
    (combined, scores), (grad_gate_w, grad_up_w, grad_down_w) = lax.scan(per_expert, start_totals, (table, gate_w, up_w, down_w))
    score_pair = scores.reshape(TOKENS, 2)
    mean_score = lax.optimization_barrier(jnp.sum(weights * score_pair, axis=1, keepdims=True))
    d_pick = (score_pair - mean_score) / pick_sum * picked * (1.0 - picked)
    dlogit = lax.optimization_barrier(jnp.sum(jnp.where(hits, d_pick[:, :, None], 0.0), axis=1))
    dnormed = combined + jnp.dot(dlogit, router_w.T, precision=highest)
    grad_router = jnp.dot(normed_rows.T, dlogit, precision=highest)
    normalized_gradient = dnormed * modulation_amplitude
    first_moment = lax.optimization_barrier(jnp.mean(normalized_gradient, axis=1, keepdims=True))
    second_moment = lax.optimization_barrier(jnp.mean(normalized_gradient * centered_scaled, axis=1, keepdims=True))
    latent_gradient = (inverse_deviation * (normalized_gradient - first_moment - centered_scaled * second_moment) + output_gradient_f32).astype(jnp.bfloat16)
    return (latent_gradient, grad_gate_w, grad_up_w, grad_down_w, grad_router)
```

```python
import jax
import jax.numpy as jnp
from jax import lax
from jax.sharding import PartitionSpec as P

SEQ = 4096

norm_eps = 1e-06
HIGHEST = lax.Precision.HIGHEST
F32 = jnp.float32
BF16 = jnp.bfloat16


def slot_targets(routes, experts, capacity):
    flat_routes = routes.reshape(-1)
    expert_ids = jnp.arange(experts, dtype=jnp.int32)
    onehot = (flat_routes[:, None] == expert_ids[None, :]).astype(jnp.int32)
    rank_run = jnp.cumsum(onehot, axis=0) - 1
    slots = flat_routes * capacity + jnp.sum(onehot * rank_run, axis=1)
    return slots.reshape(routes.shape)


def pair_swap(value):
    return lax.ppermute(value, "expert", [(0, 1), (1, 0)])


def core_sum(value):
    if lax.axis_size("expert") == 2:
        return value + pair_swap(value)
    return lax.psum(value, "expert")


def whole_features(part):
    if lax.axis_size("expert") == 2:
        other = pair_swap(part)
        first = lax.axis_index("expert") == 0
        return jnp.concatenate(
            [jnp.where(first, part, other), jnp.where(first, other, part)], axis=-1
        )
    return lax.all_gather(part, "expert", axis=part.ndim - 1, tiled=True)


def scatter_features(value):
    if lax.axis_size("expert") == 2:
        half = value.shape[-1] // 2
        low, high = value[..., :half], value[..., half:]
        first = lax.axis_index("expert") == 0
        other = pair_swap(jnp.where(first, high, low))
        return jnp.where(first, low, high).astype(F32) + other.astype(F32)
    return lax.psum_scatter(
        value, "expert", scatter_dimension=value.ndim - 1, tiled=True
    ).astype(F32)


def dp_sum(value):
    size = lax.axis_size("dp")
    step = 1
    while step < size:
        if size % (2 * step):
            return lax.psum(value, "dp")
        step *= 2
    step = 1
    while step < size:
        value = value + lax.ppermute(value, "dp", [(i, i ^ step) for i in range(size)])
        step *= 2
    return value


def all_to_all(value):
    return lax.all_to_all(value, "dp", split_axis=0, concat_axis=0, tiled=True)


def owner_view(arrived, groups, local):
    shaped = arrived.reshape((groups, local) + arrived.shape[1:])
    shaped = jnp.swapaxes(shaped, 0, 1)
    return shaped.reshape((local, groups * arrived.shape[1]) + arrived.shape[2:])


def sender_view(outgoing, groups):
    local = outgoing.shape[0]
    capacity = outgoing.shape[1] // groups
    shaped = outgoing.reshape((local, groups, capacity) + outgoing.shape[2:])
    shaped = jnp.swapaxes(shaped, 0, 1)
    return shaped.reshape((groups * local, capacity) + outgoing.shape[2:])


def selected_row(table, sample_index):
    return lax.dynamic_slice_in_dim(table, sample_index, 1, 0).astype(F32)


def split_bf16(value):
    high = value.astype(BF16)
    low = (value - high.astype(F32)).astype(BF16)
    return high, low


def per_device(
    latents, cotangent, routes, router_w, mod_shift, mod_scale, mod_gate, gate_w, up_w, down_w
):
    tok_rows, width = latents.shape
    experts = router_w.shape[1]
    local = gate_w.shape[0]
    groups = lax.axis_size("dp")
    entire_width = width * lax.axis_size("expert")
    capacity = 3 * tok_rows // experts
    slot_count = experts * capacity
    sample_index = lax.axis_index("dp") * tok_rows // SEQ

    targets = slot_targets(routes, experts, capacity)
    slot_ids = jnp.arange(slot_count, dtype=jnp.int32)
    hit0 = targets[:, 0][None, :] == slot_ids[:, None]
    hit1 = targets[:, 1][None, :] == slot_ids[:, None]
    fill = (hit0 | hit1).astype(BF16)

    def to_slots(rows_b):
        rows = jnp.dot(fill, rows_b, preferred_element_type=F32).astype(BF16)
        return rows.reshape(experts, capacity, width)

    cot = cotangent.astype(F32)
    scaled_dy = (selected_row(mod_gate, sample_index) * cot).astype(BF16)
    got_z = all_to_all(to_slots(scaled_dy))

    x = latents.astype(F32)
    sums = jnp.stack([jnp.sum(x, axis=1), jnp.sum(x * x, axis=1)])
    mean, msq = core_sum(sums) / entire_width
    inv_std = lax.rsqrt(msq - mean * mean + norm_eps)[:, None]
    xhat = (x - mean[:, None]) * inv_std
    amp = 1.0 + selected_row(mod_scale, sample_index)
    normed = xhat * amp + selected_row(mod_shift, sample_index)
    got_x = all_to_all(to_slots(normed.astype(BF16)))

    logits = core_sum(lax.dot_general(
        router_w, normed, (((0,), (1,)), ((), ())), precision=HIGHEST
    )).T
    chances = jax.nn.sigmoid(logits)
    expert_ids = jnp.arange(experts, dtype=jnp.int32)
    hits = routes[:, :, None] == expert_ids[None, None, :]
    picked = jnp.sum(jnp.where(hits, chances[:, None, :], 0.0), axis=2)
    pick_sum = jnp.sum(picked, axis=1, keepdims=True)
    weights = picked / pick_sum
    w0, w1 = weights[:, 0], weights[:, 1]
    send_w = jnp.sum(
        jnp.where(hit0, w0[None, :], 0.0) + jnp.where(hit1, w1[None, :], 0.0), axis=1
    ).astype(BF16)
    got_w = all_to_all(send_w.reshape(experts, capacity))

    rows_z = owner_view(whole_features(got_z), groups, local)
    rows_x = owner_view(whole_features(got_x), groups, local)
    slot_w = owner_view(got_w, groups, local).astype(F32)[..., None]

    down_back = jnp.einsum("esd,ehd->esh", rows_z, down_w, preferred_element_type=F32)
    gate_lin = jnp.einsum("esd,edh->esh", rows_x, gate_w, preferred_element_type=F32)
    up_lin = jnp.einsum("esd,edh->esh", rows_x, up_w, preferred_element_type=F32)
    gate_sig = jax.nn.sigmoid(gate_lin)
    gate_act = gate_lin * gate_sig
    hidden = gate_act * up_lin
    slot_score = jnp.sum(hidden * down_back, axis=-1)
    d_gate = down_back * up_lin * gate_sig * (1.0 + gate_lin * (1.0 - gate_sig))
    d_up = down_back * gate_act
    part = (
        jnp.einsum("esh,edh->esd", d_gate.astype(BF16), gate_w, preferred_element_type=F32)
        + jnp.einsum("esh,edh->esd", d_up.astype(BF16), up_w, preferred_element_type=F32)
    ).astype(BF16)
    summed = scatter_features(part).astype(BF16)

    back_scores = all_to_all(sender_view(slot_score, groups)).reshape(-1)
    back_rows = all_to_all(sender_view(summed, groups)).reshape(slot_count, width)

    gate_wt = (slot_w * d_gate).astype(BF16)
    up_wt = (slot_w * d_up).astype(BF16)
    hidden_wt = (slot_w * hidden).astype(BF16)
    grad_gate = jnp.einsum("esd,esh->edh", rows_x, gate_wt, preferred_element_type=F32)
    grad_up = jnp.einsum("esd,esh->edh", rows_x, up_wt, preferred_element_type=F32)
    grad_down = jnp.einsum("esh,esd->ehd", hidden_wt, rows_z, preferred_element_type=F32)

    score_row = back_scores[:, None]
    score = core_sum(jnp.stack([
        jnp.sum(jnp.where(hit0, score_row, 0.0), axis=0),
        jnp.sum(jnp.where(hit1, score_row, 0.0), axis=0),
    ])).T
    mean_score = jnp.sum(weights * score, axis=1, keepdims=True)
    d_pick = (score - mean_score) / pick_sum * picked * (1.0 - picked)
    dlogit = jnp.sum(jnp.where(hits, d_pick[:, :, None], 0.0), axis=1)
    grad_router = dp_sum(lax.dot_general(
        dlogit, normed, (((0,), (0,)), ((), ())), precision=HIGHEST
    )).T

    mix = jnp.where(hit0, w0[None, :], 0.0) + jnp.where(hit1, w1[None, :], 0.0)
    mix_high, mix_low = split_bf16(mix)
    contract = (((0,), (0,)), ((), ()))
    combined = lax.dot_general(
        mix_high, back_rows, contract, preferred_element_type=F32
    ) + lax.dot_general(mix_low, back_rows, contract, preferred_element_type=F32)
    dnormed = combined + lax.dot_general(
        dlogit, router_w, (((1,), (1,)), ((), ())), precision=HIGHEST
    )
    dxhat = dnormed * amp
    m_one, m_two = core_sum(
        jnp.stack([jnp.sum(dxhat, axis=1), jnp.sum(dxhat * xhat, axis=1)])
    ) / entire_width
    latent_gradient = inv_std * (dxhat - m_one[:, None] - xhat * m_two[:, None]) + cot
    return (
        latent_gradient.astype(BF16),
        grad_gate.astype(BF16),
        grad_up.astype(BF16),
        grad_down.astype(BF16),
        grad_router,
    )


def solution(mesh):
    placed = (
        P("dp", "expert"),
        P("dp", "expert"),
        P("dp", None),
        P("expert", None),
        P(None, "expert"),
        P(None, "expert"),
        P(None, "expert"),
        P("dp", None, "expert"),
        P("dp", None, "expert"),
        P("dp", "expert", None),
    )
    return jax.shard_map(
        per_device,
        mesh=mesh,
        in_specs=placed,
        out_specs=(
            P("dp", "expert"),
            P("dp", None, "expert"),
            P("dp", None, "expert"),
            P("dp", "expert", None),
            P("expert", None),
        ),
        check_vma=False,
    )
```

```python
import jax
import jax.numpy as jnp
from jax import lax
from jax.experimental import pallas as pl
from jax.experimental.pallas import tpu as pltpu
from jax.sharding import PartitionSpec as P


SEQ = 4096

norm_eps = 1e-06
HIGHEST = lax.Precision.HIGHEST
F32 = jnp.float32
BF16 = jnp.bfloat16


def slot_targets(routes, experts, capacity):
    flat_routes = routes.reshape(-1)
    expert_ids = jnp.arange(experts, dtype=jnp.int32)
    onehot = (flat_routes[:, None] == expert_ids[None, :]).astype(jnp.int32)
    rank_run = jnp.cumsum(onehot, axis=0) - 1
    slots = flat_routes * capacity + jnp.sum(onehot * rank_run, axis=1)
    return slots.reshape(routes.shape)


def pair_swap(value):
    return lax.ppermute(value, "expert", [(0, 1), (1, 0)])


def core_sum(value):
    if lax.axis_size("expert") == 2:
        return value + pair_swap(value)
    return lax.psum(value, "expert")


def whole_features(part):
    if lax.axis_size("expert") == 2:
        other = pair_swap(part)
        first = lax.axis_index("expert") == 0
        return jnp.concatenate(
            [jnp.where(first, part, other), jnp.where(first, other, part)], axis=-1
        )
    return lax.all_gather(part, "expert", axis=part.ndim - 1, tiled=True)


def scatter_features(value):
    if lax.axis_size("expert") == 2:
        half = value.shape[-1] // 2
        low, high = value[..., :half], value[..., half:]
        first = lax.axis_index("expert") == 0
        other = pair_swap(jnp.where(first, high, low))
        return jnp.where(first, low, high).astype(F32) + other.astype(F32)
    return lax.psum_scatter(
        value, "expert", scatter_dimension=value.ndim - 1, tiled=True
    ).astype(F32)


def dp_sum(value):
    size = lax.axis_size("dp")
    step = 1
    while step < size:
        if size % (2 * step):
            return lax.psum(value, "dp")
        step *= 2
    step = 1
    while step < size:
        value = value + lax.ppermute(value, "dp", [(i, i ^ step) for i in range(size)])
        step *= 2
    return value


def all_to_all(value):
    return lax.all_to_all(value, "dp", split_axis=0, concat_axis=0, tiled=True)


def owner_view(arrived, groups, local):
    shaped = arrived.reshape((groups, local) + arrived.shape[1:])
    shaped = jnp.swapaxes(shaped, 0, 1)
    return shaped.reshape((local, groups * arrived.shape[1]) + arrived.shape[2:])


def sender_view(outgoing, groups):
    local = outgoing.shape[0]
    capacity = outgoing.shape[1] // groups
    shaped = outgoing.reshape((local, groups, capacity) + outgoing.shape[2:])
    shaped = jnp.swapaxes(shaped, 0, 1)
    return shaped.reshape((groups * local, capacity) + outgoing.shape[2:])


def selected_row(table, sample_index):
    return lax.dynamic_slice_in_dim(table, sample_index, 1, 0).astype(F32)


def split_bf16(value):
    high = value.astype(BF16)
    low = (value - high.astype(F32)).astype(BF16)
    return high, low


def spread_device(
    latents, cotangent, routes, router_w, mod_shift, mod_scale, mod_gate, gate_w, up_w, down_w
):
    tok_rows, width = latents.shape
    experts = router_w.shape[1]
    local = gate_w.shape[0]
    groups = lax.axis_size("dp")
    entire_width = width * lax.axis_size("expert")
    capacity = 3 * tok_rows // experts
    slot_count = experts * capacity
    sample_index = lax.axis_index("dp") * tok_rows // SEQ

    targets = slot_targets(routes, experts, capacity)
    slot_ids = jnp.arange(slot_count, dtype=jnp.int32)
    hit0 = targets[:, 0][None, :] == slot_ids[:, None]
    hit1 = targets[:, 1][None, :] == slot_ids[:, None]
    fill = (hit0 | hit1).astype(BF16)

    def to_slots(rows_b):
        rows = jnp.dot(fill, rows_b, preferred_element_type=F32).astype(BF16)
        return rows.reshape(experts, capacity, width)

    cot = cotangent.astype(F32)
    scaled_dy = (selected_row(mod_gate, sample_index) * cot).astype(BF16)
    got_z = all_to_all(to_slots(scaled_dy))

    x = latents.astype(F32)
    sums = jnp.stack([jnp.sum(x, axis=1), jnp.sum(x * x, axis=1)])
    mean, msq = core_sum(sums) / entire_width
    inv_std = lax.rsqrt(msq - mean * mean + norm_eps)[:, None]
    xhat = (x - mean[:, None]) * inv_std
    amp = 1.0 + selected_row(mod_scale, sample_index)
    normed = xhat * amp + selected_row(mod_shift, sample_index)
    got_x = all_to_all(to_slots(normed.astype(BF16)))

    logits = core_sum(lax.dot_general(
        router_w, normed, (((0,), (1,)), ((), ())), precision=HIGHEST
    )).T
    chances = jax.nn.sigmoid(logits)
    expert_ids = jnp.arange(experts, dtype=jnp.int32)
    hits = routes[:, :, None] == expert_ids[None, None, :]
    picked = jnp.sum(jnp.where(hits, chances[:, None, :], 0.0), axis=2)
    pick_sum = jnp.sum(picked, axis=1, keepdims=True)
    weights = picked / pick_sum
    w0, w1 = weights[:, 0], weights[:, 1]
    send_w = jnp.sum(
        jnp.where(hit0, w0[None, :], 0.0) + jnp.where(hit1, w1[None, :], 0.0), axis=1
    ).astype(BF16)
    got_w = all_to_all(send_w.reshape(experts, capacity))

    rows_z = owner_view(whole_features(got_z), groups, local)
    rows_x = owner_view(whole_features(got_x), groups, local)
    slot_w = owner_view(got_w, groups, local).astype(F32)[..., None]

    down_back = jnp.einsum("esd,ehd->esh", rows_z, down_w, preferred_element_type=F32)
    gate_lin = jnp.einsum("esd,edh->esh", rows_x, gate_w, preferred_element_type=F32)
    up_lin = jnp.einsum("esd,edh->esh", rows_x, up_w, preferred_element_type=F32)
    gate_sig = jax.nn.sigmoid(gate_lin)
    gate_act = gate_lin * gate_sig
    hidden = gate_act * up_lin
    slot_score = jnp.sum(hidden * down_back, axis=-1)
    d_gate = down_back * up_lin * gate_sig * (1.0 + gate_lin * (1.0 - gate_sig))
    d_up = down_back * gate_act
    part = (
        jnp.einsum("esh,edh->esd", d_gate.astype(BF16), gate_w, preferred_element_type=F32)
        + jnp.einsum("esh,edh->esd", d_up.astype(BF16), up_w, preferred_element_type=F32)
    ).astype(BF16)
    summed = scatter_features(part).astype(BF16)

    back_scores = all_to_all(sender_view(slot_score, groups)).reshape(-1)
    back_rows = all_to_all(sender_view(summed, groups)).reshape(slot_count, width)

    gate_wt = (slot_w * d_gate).astype(BF16)
    up_wt = (slot_w * d_up).astype(BF16)
    hidden_wt = (slot_w * hidden).astype(BF16)
    grad_gate = jnp.einsum("esd,esh->edh", rows_x, gate_wt, preferred_element_type=F32)
    grad_up = jnp.einsum("esd,esh->edh", rows_x, up_wt, preferred_element_type=F32)
    grad_down = jnp.einsum("esh,esd->ehd", hidden_wt, rows_z, preferred_element_type=F32)

    score_row = back_scores[:, None]
    score = core_sum(jnp.stack([
        jnp.sum(jnp.where(hit0, score_row, 0.0), axis=0),
        jnp.sum(jnp.where(hit1, score_row, 0.0), axis=0),
    ])).T
    mean_score = jnp.sum(weights * score, axis=1, keepdims=True)
    d_pick = (score - mean_score) / pick_sum * picked * (1.0 - picked)
    dlogit = jnp.sum(jnp.where(hits, d_pick[:, :, None], 0.0), axis=1)
    grad_router = dp_sum(lax.dot_general(
        dlogit, normed, (((0,), (0,)), ((), ())), precision=HIGHEST
    )).T

    mix = jnp.where(hit0, w0[None, :], 0.0) + jnp.where(hit1, w1[None, :], 0.0)
    mix_high, mix_low = split_bf16(mix)
    contract = (((0,), (0,)), ((), ()))
    combined = lax.dot_general(
        mix_high, back_rows, contract, preferred_element_type=F32
    ) + lax.dot_general(mix_low, back_rows, contract, preferred_element_type=F32)
    dnormed = combined + lax.dot_general(
        dlogit, router_w, (((1,), (1,)), ((), ())), precision=HIGHEST
    )
    dxhat = dnormed * amp
    m_one, m_two = core_sum(
        jnp.stack([jnp.sum(dxhat, axis=1), jnp.sum(dxhat * xhat, axis=1)])
    ) / entire_width
    latent_gradient = inv_std * (dxhat - m_one[:, None] - xhat * m_two[:, None]) + cot
    return (
        latent_gradient.astype(BF16),
        grad_gate.astype(BF16),
        grad_up.astype(BF16),
        grad_down.astype(BF16),
        grad_router,
    )


FEATURE_TILE = 512


def after(value, *deps):
    return lax.optimization_barrier((value,) + deps)[0]


def dp_gather(value):
    size = lax.axis_size("dp")
    index = lax.axis_index("dp")
    value = value[None]
    step = 1
    while step < size:
        other = lax.ppermute(value, "dp", [(i, i ^ step) for i in range(size)])
        low = (index & step) == 0
        value = jnp.concatenate([jnp.where(low, value, other), jnp.where(low, other, value)])
        step *= 2
    return value


def lin(rows, weight):
    return jnp.dot(rows, weight, preferred_element_type=F32)


def lin_t(rows, weight):
    return lax.dot_general(rows, weight, (((1,), (1,)), ((), ())), preferred_element_type=F32)


def lin_rows(left, right):
    return lax.dot_general(left, right, (((0,), (0,)), ((), ())), preferred_element_type=F32)


def expert_body(
    core, own_x, oth_x, down_hbm, slot_w, coefs, router_own, router_oth, gate_hbm, up_hbm,
    part_own, part_oth, gate_wt, up_wt, hidden_wt, high, low,
    x_s, back_s, gate_s, up_s, own_s, oth_s, wt_s, sems, out_sems,
):
    width = own_x.shape[1]
    halves = [pl.ds(place * width, width) for place in range(2)]
    picked = [
        pl.ds(pl.multiple_of(((core[0] + place) % 2) * width, width), width)
        for place in range(2)
    ]

    def load(source, target, index, place):
        copy = pltpu.make_async_copy(source, target, sems.at[index, place])
        copy.start()
        return copy

    x_copies = [load(own_x, x_s.at[0], 0, 0)]
    gate_copies = [load(gate_hbm.at[picked[0]], gate_s.at[halves[0]], 1, 0)]
    x_copies.append(load(oth_x, x_s.at[1], 0, 1))
    gate_copies.append(load(gate_hbm.at[picked[1]], gate_s.at[halves[1]], 1, 1))
    up_copies = [load(up_hbm.at[picked[p]], up_s.at[halves[p]], 2, p) for p in range(2)]
    back_copy = load(down_hbm, back_s, 3, 0)

    def save(source, target, index):
        copy = pltpu.make_async_copy(source, target, out_sems.at[index])
        copy.start()
        return copy

    x_copies[0].wait()
    gate_copies[0].wait()
    gate_lin = lin(x_s[0], gate_s[:width])
    x_copies[1].wait()
    gate_copies[1].wait()
    gate_lin = gate_lin + lin(x_s[1], gate_s[width:])
    for copy in up_copies:
        copy.wait()
    up_lin = lin(x_s[0], up_s[:width]) + lin(x_s[1], up_s[width:])
    back_copy.wait()
    down_back = back_s[...]
    gate_sig = jax.nn.sigmoid(gate_lin)
    gate_act = gate_lin * gate_sig
    hidden = gate_act * up_lin
    scored = jnp.sum(hidden * down_back, axis=1, keepdims=True) * coefs[...]
    scored_b = scored.astype(BF16)
    high[...] = scored_b
    low[...] = (scored - scored_b.astype(F32)).astype(BF16)
    scale = slot_w[...]
    wt_s[0] = (scale * down_back * up_lin * gate_sig * (1.0 + gate_lin * (1.0 - gate_sig))).astype(BF16)
    wt_s[1] = (scale * down_back * gate_act).astype(BF16)
    wt_s[2] = (scale * hidden).astype(BF16)
    saves = [save(wt_s.at[k], ref, k) for k, ref in enumerate((gate_wt, up_wt, hidden_wt))]
    oth_s[...] = (
        lin_t(wt_s[0], gate_s[width:]) + lin_t(wt_s[1], up_s[width:]) + lin(scored_b, router_oth[...])
    ).astype(BF16)
    saves.append(save(oth_s, part_oth, 3))
    own_s[...] = (
        lin_t(wt_s[0], gate_s[:width]) + lin_t(wt_s[1], up_s[:width]) + lin(scored_b, router_own[...])
    ).astype(BF16)
    saves.append(save(own_s, part_own, 4))
    for copy in saves:
        copy.wait()


def expert_rows(core, own_x, oth_x, down_back, slot_w, coefs, router_own, router_oth, gate_w, up_w):
    rows, width = own_x.shape
    hidden = gate_w.shape[1]
    raw = pl.BlockSpec(memory_space=pl.ANY)
    whole = pl.BlockSpec(memory_space=pltpu.VMEM)
    wide = jax.ShapeDtypeStruct((rows, width), BF16)
    deep = jax.ShapeDtypeStruct((rows, hidden), BF16)
    narrow = jax.ShapeDtypeStruct(coefs.shape, BF16)
    return pl.pallas_call(
        expert_body,
        name="expert_rows",
        in_specs=[pl.BlockSpec(memory_space=pltpu.SMEM)] + [raw] * 3 + [whole] * 4 + [raw] * 2,
        out_specs=[raw] * 5 + [whole] * 2,
        scratch_shapes=[
            pltpu.VMEM((2, rows, width), BF16),
            pltpu.VMEM((rows, hidden), F32),
            pltpu.VMEM((2 * width, hidden), BF16),
            pltpu.VMEM((2 * width, hidden), BF16),
            pltpu.VMEM((rows, width), BF16),
            pltpu.VMEM((rows, width), BF16),
            pltpu.VMEM((3, rows, hidden), BF16),
            pltpu.SemaphoreType.DMA((4, 2)),
            pltpu.SemaphoreType.DMA((5,)),
        ],
        out_shape=[wide, wide, deep, deep, deep, narrow, narrow],
        cost_estimate=pl.CostEstimate(
            flops=16 * rows * width * hidden,
            bytes_accessed=8 * width * hidden + 8 * rows * width + 10 * rows * hidden,
            transcendentals=rows * hidden,
        ),
    )(core, own_x, oth_x, down_back, slot_w, coefs, router_own, router_oth, gate_w, up_w)


def router_body(own_x, oth_x, high, low, own, oth):
    for rows, out in ((own_x, own), (oth_x, oth)):
        out[...] = lin_rows(high[...], rows[...]) + lin_rows(low[...], rows[...])


def router_grads(own_x, oth_x, high, low):
    rows, width = own_x.shape
    experts = high.shape[1]
    out = jax.ShapeDtypeStruct((experts, width), F32)
    return pl.pallas_call(
        router_body,
        name="router_grads",
        out_shape=[out, out],
        cost_estimate=pl.CostEstimate(
            flops=8 * rows * width * experts,
            bytes_accessed=4 * rows * width,
            transcendentals=0,
        ),
    )(own_x, oth_x, high, low)


def weight_body(core, own_x, oth_x, own_z, oth_z, gate_wt, up_wt, hidden_wt, *grads):
    grad_gate, grad_up, grad_down = grads

    def write(x_rows, z_rows):
        grad_gate[...] = lin_rows(x_rows[...], gate_wt[...]).astype(BF16)
        grad_up[...] = lin_rows(x_rows[...], up_wt[...]).astype(BF16)
        grad_down[...] = lin_rows(hidden_wt[...], z_rows[...]).astype(BF16)

    @pl.when(pl.program_id(0) == 0)
    def _():
        write(own_x, own_z)

    @pl.when(pl.program_id(0) == 1)
    def _():
        write(oth_x, oth_z)


def weight_grads(core, own_x, oth_x, own_z, oth_z, gate_wt, up_wt, hidden_wt):
    rows, width = own_x.shape
    hidden = gate_wt.shape[1]
    tile = FEATURE_TILE if width % FEATURE_TILE == 0 else width
    steps = width // tile
    own = pl.BlockSpec((rows, tile), lambda h, i, core: (0, jnp.where(h == 0, i, steps - 1)))
    oth = pl.BlockSpec((rows, tile), lambda h, i, core: (0, jnp.where(h == 0, 0, i)))
    full = pl.BlockSpec((rows, hidden), lambda h, i, core: (0, 0))
    by_rows = pl.BlockSpec((tile, hidden), lambda h, i, core: (((core[0] + h) % 2) * steps + i, 0))
    by_columns = pl.BlockSpec((hidden, tile), lambda h, i, core: (0, ((core[0] + h) % 2) * steps + i))
    tall = jax.ShapeDtypeStruct((2 * width, hidden), BF16)
    return pl.pallas_call(
        weight_body,
        name="weight_grads",
        grid_spec=pltpu.PrefetchScalarGridSpec(
            num_scalar_prefetch=1,
            grid=(2, steps),
            in_specs=[own, oth, own, oth] + [full] * 3,
            out_specs=[by_rows, by_rows, by_columns],
        ),
        out_shape=[tall, tall, jax.ShapeDtypeStruct((hidden, 2 * width), BF16)],
        cost_estimate=pl.CostEstimate(
            flops=12 * rows * width * hidden,
            bytes_accessed=12 * width * hidden + 8 * rows * width + 6 * rows * hidden,
            transcendentals=0,
        ),
    )(core, own_x, oth_x, own_z, oth_z, gate_wt, up_wt, hidden_wt)


def per_device(
    latents, cotangent, routes, router_w, mod_shift, mod_scale, mod_gate, gate_w, up_w, down_w
):
    size = lax.axis_size("dp")
    if lax.axis_size("expert") != 2 or size & (size - 1) or gate_w.shape[0] != 1:
        return spread_device(
            latents, cotangent, routes, router_w, mod_shift, mod_scale, mod_gate,
            gate_w, up_w, down_w,
        )
    tok_rows, width = latents.shape
    experts = router_w.shape[1]
    entire_width = 2 * width
    capacity = 3 * tok_rows // experts
    slot_count = experts * capacity
    dp_index = lax.axis_index("dp")
    sample_index = dp_index * tok_rows // SEQ
    core = lax.axis_index("expert").astype(jnp.int32).reshape(1)
    gate_w, up_w, down_w = gate_w[0], up_w[0], down_w[0]

    expert_ids = lax.broadcasted_iota(jnp.int32, (experts, tok_rows), 0)
    named = [routes[:, k][None, :] == expert_ids for k in range(2)]
    named_b = (named[0] | named[1]).astype(BF16)
    rows_i = lax.broadcasted_iota(jnp.int32, (tok_rows, tok_rows), 0)
    cols_i = lax.broadcasted_iota(jnp.int32, (tok_rows, tok_rows), 1)
    places = lin(named_b, (rows_i < cols_i).astype(BF16)) + (expert_ids * capacity).astype(F32)
    targets = [jnp.sum(jnp.where(n, places, 0.0), axis=0) for n in named]
    slot_ids = lax.broadcasted_iota(jnp.int32, (slot_count, tok_rows), 0).astype(F32)
    fill = ((targets[0][None, :] == slot_ids) | (targets[1][None, :] == slot_ids)).astype(BF16)

    def to_slots(rows_b):
        return lin(fill, rows_b).astype(BF16).reshape(experts, capacity, width)

    cot = cotangent.astype(F32)
    scaled_dy = (selected_row(mod_gate, sample_index) * cot).astype(BF16)
    send_z = to_slots(scaled_dy)
    latents = after(latents, send_z)
    own_z = all_to_all(send_z).reshape(slot_count, width)

    x = latents.astype(F32)
    sums = jnp.stack([jnp.sum(x, axis=1), jnp.sum(x * x, axis=1)])
    mean, msq = core_sum(sums) / entire_width
    inv_std = lax.rsqrt(msq - mean * mean + norm_eps)[:, None]
    xhat = (x - mean[:, None]) * inv_std
    amp = 1.0 + selected_row(mod_scale, sample_index)
    normed = xhat * amp + selected_row(mod_shift, sample_index)
    send_x = to_slots(normed.astype(BF16))
    own_x = all_to_all(send_x).reshape(slot_count, width)

    logits = core_sum(lax.dot_general(
        router_w, normed, (((0,), (1,)), ((), ())), precision=HIGHEST
    ))
    chances = jax.nn.sigmoid(logits)
    picked = jnp.stack([jnp.sum(jnp.where(n, chances, 0.0), axis=0) for n in named])
    pick_sum = jnp.sum(picked, axis=0, keepdims=True)
    weights = picked / pick_sum
    slopes = weights[::-1] * picked * (1.0 - picked) / pick_sum
    other_ids = routes.T[::-1].astype(F32)
    slot_row = lax.broadcasted_iota(jnp.int32, (tok_rows, slot_count), 1).astype(F32)
    hits = [t[:, None] == slot_row for t in targets]

    def of_slots(pair):
        return jnp.sum(
            jnp.where(hits[0], pair[0][:, None], 0.0) + jnp.where(hits[1], pair[1][:, None], 0.0),
            axis=0,
        ).reshape(experts, capacity)

    kinds = (weights, slopes, slopes[::-1], other_ids)
    sent = jnp.concatenate([of_slots(pair) for pair in kinds], axis=1)
    arrived = lax.dynamic_index_in_dim(dp_gather(sent), dp_index, 1, keepdims=False)
    slot_w, slope, slope_other, other = [
        arrived[:, k * capacity:(k + 1) * capacity].reshape(slot_count, 1) for k in range(4)
    ]
    ids = lax.broadcasted_iota(jnp.int32, (slot_count, experts), 1).astype(F32)
    coefs = jnp.where(ids == dp_index.astype(F32), slope, 0.0) - jnp.where(
        ids == other, slope_other, 0.0
    )
    router_own = router_w.T.astype(BF16)
    router_oth = pair_swap(router_own)
    join = (hits[0] | hits[1]).astype(BF16)

    oth_z = pair_swap(own_z)
    down_own = lax.dynamic_slice_in_dim(down_w, core[0] * width, width, 1)
    down_oth = lax.dynamic_slice_in_dim(down_w, (1 - core[0]) * width, width, 1)
    down_back = lin_t(own_z, down_own) + lin_t(oth_z, down_oth)
    own_x, down_back, slot_w, coefs, join = lax.optimization_barrier(
        (own_x, down_back, slot_w, coefs, join)
    )

    oth_x = pair_swap(own_x)
    part_own, part_oth, gate_wt, up_wt, hidden_wt, high, low = expert_rows(
        core, own_x, oth_x, down_back, slot_w, coefs, router_own, router_oth, gate_w, up_w
    )
    send_back = (part_own.astype(F32) + pair_swap(part_oth).astype(F32)).astype(BF16)
    back = all_to_all(send_back.reshape(experts, capacity, width)).reshape(slot_count, width)

    router_own, router_oth = router_grads(own_x, oth_x, high, low)
    grad_gate, grad_up, grad_down = weight_grads(
        core, own_x, oth_x, own_z, oth_z, gate_wt, up_wt, hidden_wt
    )
    grad_router = dp_sum(router_own + pair_swap(router_oth)).T

    dxhat = lin(join, back) * amp
    m_one, m_two = core_sum(
        jnp.stack([jnp.sum(dxhat, axis=1), jnp.sum(dxhat * xhat, axis=1)])
    ) / entire_width
    latent_gradient = inv_std * (dxhat - m_one[:, None] - xhat * m_two[:, None]) + cot
    return (
        latent_gradient.astype(BF16), grad_gate[None], grad_up[None], grad_down[None], grad_router
    )


def solution(mesh):
    placed = (
        P("dp", "expert"),
        P("dp", "expert"),
        P("dp", None),
        P("expert", None),
        P(None, "expert"),
        P(None, "expert"),
        P(None, "expert"),
        P("dp", None, "expert"),
        P("dp", None, "expert"),
        P("dp", "expert", None),
    )
    return jax.shard_map(
        per_device,
        mesh=mesh,
        in_specs=placed,
        out_specs=(
            P("dp", "expert"),
            P("dp", None, "expert"),
            P("dp", None, "expert"),
            P("dp", "expert", None),
            P("expert", None),
        ),
        check_vma=False,
    )
```

```python
import functools

import jax
import jax.numpy as jnp
from jax import lax
from jax.experimental import pallas as pl
from jax.experimental.pallas import tpu as pltpu
from jax.sharding import PartitionSpec as P


SEQ = 4096

norm_eps = 1e-06
HIGHEST = lax.Precision.HIGHEST
F32 = jnp.float32
BF16 = jnp.bfloat16


def slot_targets(routes, experts, capacity):
    flat_routes = routes.reshape(-1)
    expert_ids = jnp.arange(experts, dtype=jnp.int32)
    onehot = (flat_routes[:, None] == expert_ids[None, :]).astype(jnp.int32)
    rank_run = jnp.cumsum(onehot, axis=0) - 1
    slots = flat_routes * capacity + jnp.sum(onehot * rank_run, axis=1)
    return slots.reshape(routes.shape)


def pair_swap(value):
    return lax.ppermute(value, "expert", [(0, 1), (1, 0)])


def core_sum(value):
    if lax.axis_size("expert") == 2:
        return value + pair_swap(value)
    return lax.psum(value, "expert")


def whole_features(part):
    if lax.axis_size("expert") == 2:
        other = pair_swap(part)
        first = lax.axis_index("expert") == 0
        return jnp.concatenate(
            [jnp.where(first, part, other), jnp.where(first, other, part)], axis=-1
        )
    return lax.all_gather(part, "expert", axis=part.ndim - 1, tiled=True)


def scatter_features(value):
    if lax.axis_size("expert") == 2:
        half = value.shape[-1] // 2
        low, high = value[..., :half], value[..., half:]
        first = lax.axis_index("expert") == 0
        other = pair_swap(jnp.where(first, high, low))
        return jnp.where(first, low, high).astype(F32) + other.astype(F32)
    return lax.psum_scatter(
        value, "expert", scatter_dimension=value.ndim - 1, tiled=True
    ).astype(F32)


def dp_sum(value):
    size = lax.axis_size("dp")
    step = 1
    while step < size:
        if size % (2 * step):
            return lax.psum(value, "dp")
        step *= 2
    step = 1
    while step < size:
        value = value + lax.ppermute(value, "dp", [(i, i ^ step) for i in range(size)])
        step *= 2
    return value


def all_to_all(value):
    return lax.all_to_all(value, "dp", split_axis=0, concat_axis=0, tiled=True)


def owner_view(arrived, groups, local):
    shaped = arrived.reshape((groups, local) + arrived.shape[1:])
    shaped = jnp.swapaxes(shaped, 0, 1)
    return shaped.reshape((local, groups * arrived.shape[1]) + arrived.shape[2:])


def sender_view(outgoing, groups):
    local = outgoing.shape[0]
    capacity = outgoing.shape[1] // groups
    shaped = outgoing.reshape((local, groups, capacity) + outgoing.shape[2:])
    shaped = jnp.swapaxes(shaped, 0, 1)
    return shaped.reshape((groups * local, capacity) + outgoing.shape[2:])


def selected_row(table, sample_index):
    return lax.dynamic_slice_in_dim(table, sample_index, 1, 0).astype(F32)


def split_bf16(value):
    high = value.astype(BF16)
    low = (value - high.astype(F32)).astype(BF16)
    return high, low


def spread_device(
    latents, cotangent, routes, router_w, mod_shift, mod_scale, mod_gate, gate_w, up_w, down_w
):
    tok_rows, width = latents.shape
    experts = router_w.shape[1]
    local = gate_w.shape[0]
    groups = lax.axis_size("dp")
    entire_width = width * lax.axis_size("expert")
    capacity = 3 * tok_rows // experts
    slot_count = experts * capacity
    sample_index = lax.axis_index("dp") * tok_rows // SEQ

    targets = slot_targets(routes, experts, capacity)
    slot_ids = jnp.arange(slot_count, dtype=jnp.int32)
    hit0 = targets[:, 0][None, :] == slot_ids[:, None]
    hit1 = targets[:, 1][None, :] == slot_ids[:, None]
    fill = (hit0 | hit1).astype(BF16)

    def to_slots(rows_b):
        rows = jnp.dot(fill, rows_b, preferred_element_type=F32).astype(BF16)
        return rows.reshape(experts, capacity, width)

    cot = cotangent.astype(F32)
    scaled_dy = (selected_row(mod_gate, sample_index) * cot).astype(BF16)
    got_z = all_to_all(to_slots(scaled_dy))

    x = latents.astype(F32)
    sums = jnp.stack([jnp.sum(x, axis=1), jnp.sum(x * x, axis=1)])
    mean, msq = core_sum(sums) / entire_width
    inv_std = lax.rsqrt(msq - mean * mean + norm_eps)[:, None]
    xhat = (x - mean[:, None]) * inv_std
    amp = 1.0 + selected_row(mod_scale, sample_index)
    normed = xhat * amp + selected_row(mod_shift, sample_index)
    got_x = all_to_all(to_slots(normed.astype(BF16)))

    logits = core_sum(lax.dot_general(
        router_w, normed, (((0,), (1,)), ((), ())), precision=HIGHEST
    )).T
    chances = jax.nn.sigmoid(logits)
    expert_ids = jnp.arange(experts, dtype=jnp.int32)
    hits = routes[:, :, None] == expert_ids[None, None, :]
    picked = jnp.sum(jnp.where(hits, chances[:, None, :], 0.0), axis=2)
    pick_sum = jnp.sum(picked, axis=1, keepdims=True)
    weights = picked / pick_sum
    w0, w1 = weights[:, 0], weights[:, 1]
    send_w = jnp.sum(
        jnp.where(hit0, w0[None, :], 0.0) + jnp.where(hit1, w1[None, :], 0.0), axis=1
    ).astype(BF16)
    got_w = all_to_all(send_w.reshape(experts, capacity))

    rows_z = owner_view(whole_features(got_z), groups, local)
    rows_x = owner_view(whole_features(got_x), groups, local)
    slot_w = owner_view(got_w, groups, local).astype(F32)[..., None]

    down_back = jnp.einsum("esd,ehd->esh", rows_z, down_w, preferred_element_type=F32)
    gate_lin = jnp.einsum("esd,edh->esh", rows_x, gate_w, preferred_element_type=F32)
    up_lin = jnp.einsum("esd,edh->esh", rows_x, up_w, preferred_element_type=F32)
    gate_sig = jax.nn.sigmoid(gate_lin)
    gate_act = gate_lin * gate_sig
    hidden = gate_act * up_lin
    slot_score = jnp.sum(hidden * down_back, axis=-1)
    d_gate = down_back * up_lin * gate_sig * (1.0 + gate_lin * (1.0 - gate_sig))
    d_up = down_back * gate_act
    part = (
        jnp.einsum("esh,edh->esd", d_gate.astype(BF16), gate_w, preferred_element_type=F32)
        + jnp.einsum("esh,edh->esd", d_up.astype(BF16), up_w, preferred_element_type=F32)
    ).astype(BF16)
    summed = scatter_features(part).astype(BF16)

    back_scores = all_to_all(sender_view(slot_score, groups)).reshape(-1)
    back_rows = all_to_all(sender_view(summed, groups)).reshape(slot_count, width)

    gate_wt = (slot_w * d_gate).astype(BF16)
    up_wt = (slot_w * d_up).astype(BF16)
    hidden_wt = (slot_w * hidden).astype(BF16)
    grad_gate = jnp.einsum("esd,esh->edh", rows_x, gate_wt, preferred_element_type=F32)
    grad_up = jnp.einsum("esd,esh->edh", rows_x, up_wt, preferred_element_type=F32)
    grad_down = jnp.einsum("esh,esd->ehd", hidden_wt, rows_z, preferred_element_type=F32)

    score_row = back_scores[:, None]
    score = core_sum(jnp.stack([
        jnp.sum(jnp.where(hit0, score_row, 0.0), axis=0),
        jnp.sum(jnp.where(hit1, score_row, 0.0), axis=0),
    ])).T
    mean_score = jnp.sum(weights * score, axis=1, keepdims=True)
    d_pick = (score - mean_score) / pick_sum * picked * (1.0 - picked)
    dlogit = jnp.sum(jnp.where(hits, d_pick[:, :, None], 0.0), axis=1)
    grad_router = dp_sum(lax.dot_general(
        dlogit, normed, (((0,), (0,)), ((), ())), precision=HIGHEST
    )).T

    mix = jnp.where(hit0, w0[None, :], 0.0) + jnp.where(hit1, w1[None, :], 0.0)
    mix_high, mix_low = split_bf16(mix)
    contract = (((0,), (0,)), ((), ()))
    combined = lax.dot_general(
        mix_high, back_rows, contract, preferred_element_type=F32
    ) + lax.dot_general(mix_low, back_rows, contract, preferred_element_type=F32)
    dnormed = combined + lax.dot_general(
        dlogit, router_w, (((1,), (1,)), ((), ())), precision=HIGHEST
    )
    dxhat = dnormed * amp
    m_one, m_two = core_sum(
        jnp.stack([jnp.sum(dxhat, axis=1), jnp.sum(dxhat * xhat, axis=1)])
    ) / entire_width
    latent_gradient = inv_std * (dxhat - m_one[:, None] - xhat * m_two[:, None]) + cot
    return (
        latent_gradient.astype(BF16),
        grad_gate.astype(BF16),
        grad_up.astype(BF16),
        grad_down.astype(BF16),
        grad_router,
    )


FEATURE_TILE = 512


def after(value, *deps):
    return lax.optimization_barrier((value,) + deps)[0]


def dp_total(value):
    size = lax.axis_size("dp")
    if size % 4:
        return dp_sum(value)
    step = 1
    while step < size:
        far = 3 if step * 2 < size else 1
        others = []
        for k in range(1, far + 1):
            others.append(
                lax.ppermute(value, "dp", [(i, i ^ (step * k)) for i in range(size)])
            )
        value = value + others[0]
        if far == 3:
            value = value + (others[1] + others[2])
        step *= far + 1
    return value


def dp_exchange(value):
    size = lax.axis_size("dp")
    index = lax.axis_index("dp")
    step = 1
    while step < size:
        clear = (index & step) == 0
        pairs = value.reshape(size // 2, 2, -1)
        low, high = pairs[:, 0], pairs[:, 1]
        kept, sent = jnp.where(clear, low, high), jnp.where(clear, high, low)
        other = lax.ppermute(sent, "dp", [(i, i ^ step) for i in range(size)])
        value = jnp.concatenate([jnp.where(clear, kept, other), jnp.where(clear, other, kept)])
        step *= 2
    return value


def lin(rows, weight):
    return jnp.dot(rows, weight, preferred_element_type=F32)


def lin_t(rows, weight):
    return lax.dot_general(rows, weight, (((1,), (1,)), ((), ())), preferred_element_type=F32)


def lin_rows(left, right):
    return lax.dot_general(left, right, (((0,), (0,)), ((), ())), preferred_element_type=F32)


def expert_body(
    core, own, oth, slot_w, coefs, router_own, router_oth, down_hbm, gate_hbm, up_hbm,
    part_own, part_oth, gate_wt, up_wt, hidden_wt, high, low,
    x_s, z_s, down_s, gate_s, up_s, own_s, oth_s, wt_s, row_sems, sems, out_sems,
):
    groups, chunk, width = x_s.shape[1:]
    rows = groups * chunk

    def start(source, target, sem):
        copy = pltpu.make_async_copy(source, target, sem)
        copy.start()
        return copy

    def arrived(kind, scratch):
        return [
            start(ref.at[:, pl.ds(kind * chunk, chunk)], scratch.at[place], row_sems.at[kind, place])
            for place, ref in enumerate((own, oth))
        ]

    def halves(index, hbm, scratch):
        copies = []
        for place in range(2):
            first = pl.multiple_of(((core[0] + place) % 2) * width, width)
            source = hbm.at[:, pl.ds(first, width)] if index == 0 else hbm.at[pl.ds(first, width)]
            copies.append(start(source, scratch.at[place], sems.at[index, place]))
        return copies

    z_copies, down_copies = arrived(1, z_s), halves(0, down_hbm, down_s)
    x_copies, gate_copies = arrived(0, x_s), halves(1, gate_hbm, gate_s)
    up_copies = halves(2, up_hbm, up_s)

    def rows_of(scratch, place):
        return scratch[place].reshape(rows, width)

    def total(product, scratch, copies, weight, weight_copies):
        parts = []
        for place in range(2):
            for copy in (copies[place], weight_copies[place]):
                if copy is not None:
                    copy.wait()
            parts.append(product(rows_of(scratch, place), weight[place]))
        return parts[0] + parts[1]

    down_back = total(lin_t, z_s, z_copies, down_s, down_copies)
    gate_lin = total(lin, x_s, x_copies, gate_s, gate_copies)
    gate_sig = jax.nn.sigmoid(gate_lin)
    up_lin = total(lin, x_s, (None, None), up_s, up_copies)
    gate_act = gate_lin * gate_sig
    hidden = gate_act * up_lin
    scored = jnp.sum(hidden * down_back, axis=1, keepdims=True) * coefs[...]
    scored_b = scored.astype(BF16)
    high[...] = scored_b
    low[...] = (scored - scored_b.astype(F32)).astype(BF16)
    back = slot_w[...] * down_back
    wt_s[0] = (back * up_lin * gate_sig * (1.0 + gate_lin * (1.0 - gate_sig))).astype(BF16)
    wt_s[1] = (back * gate_act).astype(BF16)
    saves = []
    for place, router, scratch, out in ((1, router_oth, oth_s, part_oth), (0, router_own, own_s, part_own)):
        scratch[...] = (
            lin_t(wt_s[0], gate_s[place]) + lin_t(wt_s[1], up_s[place]) + lin(scored_b, router[...])
        ).astype(BF16)
        saves.append(start(scratch, out, out_sems.at[3 + place]))
        if place == 1:
            wt_s[2] = (slot_w[...] * hidden).astype(BF16)
            for k, ref in enumerate((gate_wt, up_wt, hidden_wt)):
                saves.append(start(wt_s.at[k], ref, out_sems.at[k]))
    for copy in saves:
        copy.wait()


def expert_rows(core, own, oth, slot_w, coefs, router_own, router_oth, down_w, gate_w, up_w):
    groups, span, width = own.shape
    chunk = span // 2
    rows = groups * chunk
    hidden = gate_w.shape[1]
    wide = jax.ShapeDtypeStruct((rows, width), BF16)
    deep = jax.ShapeDtypeStruct((rows, hidden), BF16)
    narrow = jax.ShapeDtypeStruct(coefs.shape, BF16)
    whole = pl.BlockSpec(memory_space=pltpu.VMEM)
    raw = pl.BlockSpec(memory_space=pl.ANY)
    return pl.pallas_call(
        expert_body,
        name="expert_rows",
        in_specs=[pl.BlockSpec(memory_space=pltpu.SMEM)] + [raw] * 2 + [whole] * 4 + [raw] * 3,
        out_specs=[raw] * 5 + [whole] * 2,
        scratch_shapes=[
            pltpu.VMEM((2, groups, chunk, width), BF16),
            pltpu.VMEM((2, groups, chunk, width), BF16),
            pltpu.VMEM((2, hidden, width), BF16),
            pltpu.VMEM((2, width, hidden), BF16),
            pltpu.VMEM((2, width, hidden), BF16),
            pltpu.VMEM((rows, width), BF16),
            pltpu.VMEM((rows, width), BF16),
            pltpu.VMEM((3, rows, hidden), BF16),
            pltpu.SemaphoreType.DMA((2, 2)),
            pltpu.SemaphoreType.DMA((3, 2)),
            pltpu.SemaphoreType.DMA((5,)),
        ],
        out_shape=[wide, wide, deep, deep, deep, narrow, narrow],
        cost_estimate=pl.CostEstimate(
            flops=20 * rows * width * hidden,
            bytes_accessed=12 * width * hidden + 12 * rows * width + 6 * rows * hidden,
            transcendentals=rows * hidden,
        ),
    )(core, own, oth, slot_w, coefs, router_own, router_oth, down_w, gate_w, up_w)


def flat(ref):
    groups, chunk, width = ref.shape
    return ref[...].reshape(groups * chunk, width)


def router_body(own_1, oth_1, own_2, oth_2, high_1, low_1, high_2, low_2, own, oth):
    for one, two, out in ((own_1, own_2, own), (oth_1, oth_2, oth)):
        x_1, x_2 = flat(one), flat(two)
        out[...] = (
            lin_rows(high_1[...], x_1) + lin_rows(low_1[...], x_1)
            + lin_rows(high_2[...], x_2) + lin_rows(low_2[...], x_2)
        )


def router_grads(own_1, oth_1, own_2, oth_2, *scores):
    groups, _, width = own_1.shape
    experts = scores[0].shape[1]
    rows = scores[0].shape[0] + scores[2].shape[0]
    tile = FEATURE_TILE if width % FEATURE_TILE == 0 else width
    out = jax.ShapeDtypeStruct((experts, width), F32)
    blocks = [
        pl.BlockSpec((groups, ref.shape[1] // 2, tile), lambda i: (0, 0, i))
        for ref in (own_1, oth_1, own_2, oth_2)
    ]
    full = [pl.BlockSpec(score.shape, lambda i: (0, 0)) for score in scores]
    return pl.pallas_call(
        router_body,
        name="router_grads",
        grid=(width // tile,),
        in_specs=blocks + full,
        out_specs=[pl.BlockSpec((experts, tile), lambda i: (0, i))] * 2,
        out_shape=[out, out],
        cost_estimate=pl.CostEstimate(
            flops=8 * rows * width * experts,
            bytes_accessed=4 * rows * width,
            transcendentals=0,
        ),
    )(own_1, oth_1, own_2, oth_2, *scores)


def weight_body(
    core, x_1, z_1, x_2, z_2, gate_1, up_1, hidden_1, gate_2, up_2, hidden_2, *refs
):
    grad_gate, grad_up, grad_down = refs[-3:]
    first, second = flat(x_1), flat(x_2)
    grad_gate[...] = (lin_rows(first, gate_1[...]) + lin_rows(second, gate_2[...])).astype(BF16)
    grad_up[...] = (lin_rows(first, up_1[...]) + lin_rows(second, up_2[...])).astype(BF16)
    grad_down[...] = (
        lin_rows(hidden_1[...], flat(z_1)) + lin_rows(hidden_2[...], flat(z_2))
    ).astype(BF16)


def weight_grads(core, place, part_1, part_2, weighted, begun=()):
    groups, _, width = part_1.shape
    hidden = weighted[0].shape[1]
    rows = weighted[0].shape[0] + weighted[3].shape[0]
    tile = FEATURE_TILE if width % FEATURE_TILE == 0 else width
    steps = width // tile

    def block(ref, kind):
        return pl.BlockSpec(
            (groups, ref.shape[1] // 2, tile), lambda i, core: (0, kind, i)
        )

    blocks = [block(ref, kind) for ref in (part_1, part_2) for kind in range(2)]
    full = [pl.BlockSpec(value.shape, lambda i, core: (0, 0)) for value in weighted]
    raw = [pl.BlockSpec(memory_space=pl.ANY)] * len(begun)
    by_rows = pl.BlockSpec((tile, hidden), lambda i, core: (((core[0] + place) % 2) * steps + i, 0))
    by_columns = pl.BlockSpec((hidden, tile), lambda i, core: (0, ((core[0] + place) % 2) * steps + i))
    tall = jax.ShapeDtypeStruct((2 * width, hidden), BF16)
    return pl.pallas_call(
        weight_body,
        name="weight_grads",
        grid_spec=pltpu.PrefetchScalarGridSpec(
            num_scalar_prefetch=1,
            grid=(steps,),
            in_specs=blocks + full + raw,
            out_specs=[by_rows, by_rows, by_columns],
        ),
        out_shape=[tall, tall, jax.ShapeDtypeStruct((hidden, 2 * width), BF16)],
        input_output_aliases={11 + k: k for k in range(len(begun))},
        cost_estimate=pl.CostEstimate(
            flops=6 * rows * width * hidden,
            bytes_accessed=6 * width * hidden + 4 * rows * width + 6 * rows * hidden,
            transcendentals=0,
        ),
    )(core, part_1, part_1, part_2, part_2, *weighted, *begun)


FILL_BYTES = 24 * 2**20


def fill_body(first, targets, x_rows, z_rows, out):
    experts, span, width = out.shape
    chunk = span // 2
    capacity = 3 * targets.shape[1] // experts
    rows = experts * chunk
    index = lax.broadcasted_iota(jnp.int32, (rows, targets.shape[1]), 0)
    ids = (index // chunk * capacity + index % chunk + first).astype(F32)
    hit = (targets[0:1, :] == ids) | (targets[1:2, :] == ids)
    fill = jnp.where(hit, 1.0, 0.0).astype(BF16)
    out[:, :chunk, :] = lin(fill, x_rows[...]).astype(BF16).reshape(experts, chunk, width)
    out[:, chunk:, :] = lin(fill, z_rows[...]).astype(BF16).reshape(experts, chunk, width)


def fill_slots(targets, x_rows, z_rows, experts, first, chunk):
    width = x_rows.shape[1]
    return pl.pallas_call(
        functools.partial(fill_body, first),
        name="fill_slots",
        compiler_params=pltpu.CompilerParams(vmem_limit_bytes=FILL_BYTES),
        out_shape=jax.ShapeDtypeStruct((experts, 2 * chunk, width), BF16),
    )(targets, x_rows, z_rows)


def per_device(
    latents, cotangent, routes, router_w, mod_shift, mod_scale, mod_gate, gate_w, up_w, down_w
):
    size = lax.axis_size("dp")
    if lax.axis_size("expert") != 2 or size & (size - 1) or gate_w.shape[0] != 1 or latents.shape[0] % 256:
        return spread_device(
            latents, cotangent, routes, router_w, mod_shift, mod_scale, mod_gate,
            gate_w, up_w, down_w,
        )
    tok_rows, width = latents.shape
    experts = router_w.shape[1]
    entire_width = 2 * width
    capacity = 3 * tok_rows // experts
    slot_count = experts * capacity
    dp_index = lax.axis_index("dp")
    sample_index = dp_index * tok_rows // SEQ
    core = lax.axis_index("expert").astype(jnp.int32).reshape(1)
    gate_w, up_w, down_w = gate_w[0], up_w[0], down_w[0]

    expert_ids = lax.broadcasted_iota(jnp.int32, (experts, tok_rows), 0)
    named = [routes[:, k][None, :] == expert_ids for k in range(2)]
    named_b = (named[0] | named[1]).astype(BF16)
    rows_i = lax.broadcasted_iota(jnp.int32, (tok_rows, tok_rows), 0)
    cols_i = lax.broadcasted_iota(jnp.int32, (tok_rows, tok_rows), 1)
    places = lin(named_b, (rows_i < cols_i).astype(BF16)) + (expert_ids * capacity).astype(F32)
    targets = [jnp.sum(jnp.where(n, places, 0.0), axis=0) for n in named]
    first = capacity // 3 * 2
    parts = ((0, first), (first, capacity - first))

    def slot_of(index, first, length):
        return (index // length * capacity + index % length + first).astype(F32)

    cot = cotangent.astype(F32)
    scaled_dy = (selected_row(mod_gate, sample_index) * cot).astype(BF16)
    x = latents.astype(F32)
    sums = jnp.stack([jnp.sum(x, axis=1), jnp.sum(x * x, axis=1)])
    mean, msq = core_sum(sums) / entire_width
    inv_std = lax.rsqrt(msq - mean * mean + norm_eps)[:, None]
    xhat = (x - mean[:, None]) * inv_std
    amp = 1.0 + selected_row(mod_scale, sample_index)
    normed = xhat * amp + selected_row(mod_shift, sample_index)
    normed_b = normed.astype(BF16)
    second = capacity - first
    send_1 = fill_slots(jnp.stack(targets), normed_b, scaled_dy, experts, 0, first)
    send_2 = fill_slots(
        after(jnp.stack(targets), send_1), normed_b, scaled_dy, experts, first, second
    )
    own_1 = all_to_all(send_1)
    own_2 = all_to_all(send_2)

    logits = core_sum(lax.dot_general(
        router_w, after(normed, send_1), (((0,), (1,)), ((), ())), precision=HIGHEST
    ))
    chances = jax.nn.sigmoid(logits)
    picked = jnp.stack([jnp.sum(jnp.where(n, chances, 0.0), axis=0) for n in named])
    pick_sum = jnp.sum(picked, axis=0, keepdims=True)
    weights = picked / pick_sum
    slopes = weights[::-1] * picked * (1.0 - picked) / pick_sum
    other_ids = routes.T[::-1].astype(F32)
    slot_row = lax.broadcasted_iota(jnp.int32, (tok_rows, slot_count), 1).astype(F32)
    hits = [t[:, None] == slot_row for t in targets]

    def of_slots(pair):
        return jnp.sum(
            jnp.where(hits[0], pair[0][:, None], 0.0) + jnp.where(hits[1], pair[1][:, None], 0.0),
            axis=0,
        ).reshape(experts, capacity)

    kinds = (weights, slopes, slopes[::-1], other_ids)
    sent = jnp.concatenate([of_slots(pair) for pair in kinds], axis=1)
    arrived = dp_exchange(sent)
    columns = []
    for start, length in parts:
        rows = experts * length
        ids = lax.broadcasted_iota(jnp.int32, (rows, experts), 1).astype(F32)
        slot_w, slope, slope_other, other = [
            arrived[:, k * capacity + start:k * capacity + start + length].reshape(rows, 1)
            for k in range(4)
        ]
        coefs = jnp.where(ids == dp_index.astype(F32), slope, 0.0) - jnp.where(
            ids == other, slope_other, 0.0
        )
        columns.append((slot_w, coefs))
    router_own = router_w.T.astype(BF16)
    router_oth = pair_swap(after(router_own, send_1))
    joins = []
    for start, length in parts:
        ids = slot_of(
            lax.broadcasted_iota(jnp.int32, (tok_rows, experts * length), 1), start, length
        )
        joins.append(((targets[0][:, None] == ids) | (targets[1][:, None] == ids)).astype(BF16))

    oth_1 = pair_swap(own_1)
    part_own, part_oth, gate_1, up_1, hidden_1, high_1, low_1 = expert_rows(
        core, own_1, oth_1, *columns[0], router_own, router_oth, down_w, gate_w, up_w
    )
    back_1 = (part_own.astype(F32) + pair_swap(part_oth).astype(F32)).astype(BF16)
    back_1 = all_to_all(after(back_1, own_2).reshape(experts, first, width))
    oth_2 = pair_swap(own_2)
    part_own, part_oth, gate_2, up_2, hidden_2, high_2, low_2 = expert_rows(
        core, own_2, oth_2, *columns[1], router_own, router_oth, down_w, gate_w, up_w
    )
    back_2 = (part_own.astype(F32) + pair_swap(part_oth).astype(F32)).astype(BF16)
    weighted = (gate_1, up_1, hidden_1, gate_2, up_2, hidden_2)
    begun = weight_grads(core, 0, after(own_1, back_2), own_2, weighted)
    back_2 = all_to_all(after(back_2, back_1).reshape(experts, second, width))

    router_own, router_oth = router_grads(own_1, oth_1, own_2, oth_2, high_1, low_1, high_2, low_2)
    grad_gate, grad_up, grad_down = weight_grads(
        core, 1, oth_1, oth_2, weighted, begun
    )
    grad_router = dp_total(router_own + pair_swap(router_oth)).T

    combined = lin(joins[0], back_1.reshape(-1, width))
    dxhat = (combined + lin(joins[1], back_2.reshape(-1, width))) * amp
    m_one, m_two = core_sum(
        jnp.stack([jnp.sum(dxhat, axis=1), jnp.sum(dxhat * xhat, axis=1)])
    ) / entire_width
    latent_gradient = inv_std * (dxhat - m_one[:, None] - xhat * m_two[:, None]) + cot
    return (
        latent_gradient.astype(BF16), grad_gate[None], grad_up[None], grad_down[None], grad_router
    )


def solution(mesh):
    placed = (
        P("dp", "expert"),
        P("dp", "expert"),
        P("dp", None),
        P("expert", None),
        P(None, "expert"),
        P(None, "expert"),
        P(None, "expert"),
        P("dp", None, "expert"),
        P("dp", None, "expert"),
        P("dp", "expert", None),
    )
    return jax.shard_map(
        per_device,
        mesh=mesh,
        in_specs=placed,
        out_specs=(
            P("dp", "expert"),
            P("dp", None, "expert"),
            P("dp", None, "expert"),
            P("dp", "expert", None),
            P("expert", None),
        ),
        check_vma=False,
    )
```

```python
import functools

import jax
import jax.numpy as jnp
from jax import lax
from jax.experimental import pallas as pl
from jax.experimental.pallas import tpu as pltpu
from jax.sharding import PartitionSpec as P


SEQ = 4096

norm_eps = 1e-06
HIGHEST = lax.Precision.HIGHEST
F32 = jnp.float32
BF16 = jnp.bfloat16


def slot_targets(routes, experts, capacity):
    flat_routes = routes.reshape(-1)
    expert_ids = jnp.arange(experts, dtype=jnp.int32)
    onehot = (flat_routes[:, None] == expert_ids[None, :]).astype(jnp.int32)
    rank_run = jnp.cumsum(onehot, axis=0) - 1
    slots = flat_routes * capacity + jnp.sum(onehot * rank_run, axis=1)
    return slots.reshape(routes.shape)


def pair_swap(value):
    return lax.ppermute(value, "expert", [(0, 1), (1, 0)])


def core_sum(value):
    if lax.axis_size("expert") == 2:
        return value + pair_swap(value)
    return lax.psum(value, "expert")


def whole_features(part):
    if lax.axis_size("expert") == 2:
        other = pair_swap(part)
        first = lax.axis_index("expert") == 0
        return jnp.concatenate(
            [jnp.where(first, part, other), jnp.where(first, other, part)], axis=-1
        )
    return lax.all_gather(part, "expert", axis=part.ndim - 1, tiled=True)


def scatter_features(value):
    if lax.axis_size("expert") == 2:
        half = value.shape[-1] // 2
        low, high = value[..., :half], value[..., half:]
        first = lax.axis_index("expert") == 0
        other = pair_swap(jnp.where(first, high, low))
        return jnp.where(first, low, high).astype(F32) + other.astype(F32)
    return lax.psum_scatter(
        value, "expert", scatter_dimension=value.ndim - 1, tiled=True
    ).astype(F32)


def dp_sum(value):
    size = lax.axis_size("dp")
    step = 1
    while step < size:
        if size % (2 * step):
            return lax.psum(value, "dp")
        step *= 2
    step = 1
    while step < size:
        value = value + lax.ppermute(value, "dp", [(i, i ^ step) for i in range(size)])
        step *= 2
    return value


def all_to_all(value):
    return lax.all_to_all(value, "dp", split_axis=0, concat_axis=0, tiled=True)


def owner_view(arrived, groups, local):
    shaped = arrived.reshape((groups, local) + arrived.shape[1:])
    shaped = jnp.swapaxes(shaped, 0, 1)
    return shaped.reshape((local, groups * arrived.shape[1]) + arrived.shape[2:])


def sender_view(outgoing, groups):
    local = outgoing.shape[0]
    capacity = outgoing.shape[1] // groups
    shaped = outgoing.reshape((local, groups, capacity) + outgoing.shape[2:])
    shaped = jnp.swapaxes(shaped, 0, 1)
    return shaped.reshape((groups * local, capacity) + outgoing.shape[2:])


def selected_row(table, sample_index):
    return lax.dynamic_slice_in_dim(table, sample_index, 1, 0).astype(F32)


def split_bf16(value):
    high = value.astype(BF16)
    low = (value - high.astype(F32)).astype(BF16)
    return high, low


def spread_device(
    latents, cotangent, routes, router_w, mod_shift, mod_scale, mod_gate, gate_w, up_w, down_w
):
    tok_rows, width = latents.shape
    experts = router_w.shape[1]
    local = gate_w.shape[0]
    groups = lax.axis_size("dp")
    entire_width = width * lax.axis_size("expert")
    capacity = 3 * tok_rows // experts
    slot_count = experts * capacity
    sample_index = lax.axis_index("dp") * tok_rows // SEQ

    targets = slot_targets(routes, experts, capacity)
    slot_ids = jnp.arange(slot_count, dtype=jnp.int32)
    hit0 = targets[:, 0][None, :] == slot_ids[:, None]
    hit1 = targets[:, 1][None, :] == slot_ids[:, None]
    fill = (hit0 | hit1).astype(BF16)

    def to_slots(rows_b):
        rows = jnp.dot(fill, rows_b, preferred_element_type=F32).astype(BF16)
        return rows.reshape(experts, capacity, width)

    cot = cotangent.astype(F32)
    scaled_dy = (selected_row(mod_gate, sample_index) * cot).astype(BF16)
    got_z = all_to_all(to_slots(scaled_dy))

    x = latents.astype(F32)
    sums = jnp.stack([jnp.sum(x, axis=1), jnp.sum(x * x, axis=1)])
    mean, msq = core_sum(sums) / entire_width
    inv_std = lax.rsqrt(msq - mean * mean + norm_eps)[:, None]
    xhat = (x - mean[:, None]) * inv_std
    amp = 1.0 + selected_row(mod_scale, sample_index)
    normed = xhat * amp + selected_row(mod_shift, sample_index)
    got_x = all_to_all(to_slots(normed.astype(BF16)))

    logits = core_sum(lax.dot_general(
        router_w, normed, (((0,), (1,)), ((), ())), precision=HIGHEST
    )).T
    chances = jax.nn.sigmoid(logits)
    expert_ids = jnp.arange(experts, dtype=jnp.int32)
    hits = routes[:, :, None] == expert_ids[None, None, :]
    picked = jnp.sum(jnp.where(hits, chances[:, None, :], 0.0), axis=2)
    pick_sum = jnp.sum(picked, axis=1, keepdims=True)
    weights = picked / pick_sum
    w0, w1 = weights[:, 0], weights[:, 1]
    send_w = jnp.sum(
        jnp.where(hit0, w0[None, :], 0.0) + jnp.where(hit1, w1[None, :], 0.0), axis=1
    ).astype(BF16)
    got_w = all_to_all(send_w.reshape(experts, capacity))

    rows_z = owner_view(whole_features(got_z), groups, local)
    rows_x = owner_view(whole_features(got_x), groups, local)
    slot_w = owner_view(got_w, groups, local).astype(F32)[..., None]

    down_back = jnp.einsum("esd,ehd->esh", rows_z, down_w, preferred_element_type=F32)
    gate_lin = jnp.einsum("esd,edh->esh", rows_x, gate_w, preferred_element_type=F32)
    up_lin = jnp.einsum("esd,edh->esh", rows_x, up_w, preferred_element_type=F32)
    gate_sig = jax.nn.sigmoid(gate_lin)
    gate_act = gate_lin * gate_sig
    hidden = gate_act * up_lin
    slot_score = jnp.sum(hidden * down_back, axis=-1)
    d_gate = down_back * up_lin * gate_sig * (1.0 + gate_lin * (1.0 - gate_sig))
    d_up = down_back * gate_act
    part = (
        jnp.einsum("esh,edh->esd", d_gate.astype(BF16), gate_w, preferred_element_type=F32)
        + jnp.einsum("esh,edh->esd", d_up.astype(BF16), up_w, preferred_element_type=F32)
    ).astype(BF16)
    summed = scatter_features(part).astype(BF16)

    back_scores = all_to_all(sender_view(slot_score, groups)).reshape(-1)
    back_rows = all_to_all(sender_view(summed, groups)).reshape(slot_count, width)

    gate_wt = (slot_w * d_gate).astype(BF16)
    up_wt = (slot_w * d_up).astype(BF16)
    hidden_wt = (slot_w * hidden).astype(BF16)
    grad_gate = jnp.einsum("esd,esh->edh", rows_x, gate_wt, preferred_element_type=F32)
    grad_up = jnp.einsum("esd,esh->edh", rows_x, up_wt, preferred_element_type=F32)
    grad_down = jnp.einsum("esh,esd->ehd", hidden_wt, rows_z, preferred_element_type=F32)

    score_row = back_scores[:, None]
    score = core_sum(jnp.stack([
        jnp.sum(jnp.where(hit0, score_row, 0.0), axis=0),
        jnp.sum(jnp.where(hit1, score_row, 0.0), axis=0),
    ])).T
    mean_score = jnp.sum(weights * score, axis=1, keepdims=True)
    d_pick = (score - mean_score) / pick_sum * picked * (1.0 - picked)
    dlogit = jnp.sum(jnp.where(hits, d_pick[:, :, None], 0.0), axis=1)
    grad_router = dp_sum(lax.dot_general(
        dlogit, normed, (((0,), (0,)), ((), ())), precision=HIGHEST
    )).T

    mix = jnp.where(hit0, w0[None, :], 0.0) + jnp.where(hit1, w1[None, :], 0.0)
    mix_high, mix_low = split_bf16(mix)
    contract = (((0,), (0,)), ((), ()))
    combined = lax.dot_general(
        mix_high, back_rows, contract, preferred_element_type=F32
    ) + lax.dot_general(mix_low, back_rows, contract, preferred_element_type=F32)
    dnormed = combined + lax.dot_general(
        dlogit, router_w, (((1,), (1,)), ((), ())), precision=HIGHEST
    )
    dxhat = dnormed * amp
    m_one, m_two = core_sum(
        jnp.stack([jnp.sum(dxhat, axis=1), jnp.sum(dxhat * xhat, axis=1)])
    ) / entire_width
    latent_gradient = inv_std * (dxhat - m_one[:, None] - xhat * m_two[:, None]) + cot
    return (
        latent_gradient.astype(BF16),
        grad_gate.astype(BF16),
        grad_up.astype(BF16),
        grad_down.astype(BF16),
        grad_router,
    )


FEATURE_TILE = 512


def after(value, *deps):
    return lax.optimization_barrier((value,) + deps)[0]


def dp_total(value):
    size = lax.axis_size("dp")
    if size % 4:
        return dp_sum(value)
    step = 1
    while step < size:
        far = 3 if step == 1 else 1
        others = []
        for k in range(1, far + 1):
            others.append(
                lax.ppermute(value, "dp", [(i, i ^ (step * k)) for i in range(size)])
            )
        value = value + others[0]
        if far == 3:
            value = value + (others[1] + others[2])
        step *= far + 1
    return value


def dp_exchange(value):
    size = lax.axis_size("dp")
    index = lax.axis_index("dp")
    step = 1
    while step < size:
        clear = (index & step) == 0
        pairs = value.reshape(size // 2, 2, -1)
        low, high = pairs[:, 0], pairs[:, 1]
        kept, sent = jnp.where(clear, low, high), jnp.where(clear, high, low)
        other = lax.ppermute(sent, "dp", [(i, i ^ step) for i in range(size)])
        value = jnp.concatenate([jnp.where(clear, kept, other), jnp.where(clear, other, kept)])
        step *= 2
    return value


def lin(rows, weight):
    return jnp.dot(rows, weight, preferred_element_type=F32)


def lin_t(rows, weight):
    return lax.dot_general(rows, weight, (((1,), (1,)), ((), ())), preferred_element_type=F32)


def lin_rows(left, right):
    return lax.dot_general(left, right, (((0,), (0,)), ((), ())), preferred_element_type=F32)


def expert_body(
    core, own, oth, slot_w, coefs, router_own, router_oth, down_hbm, gate_hbm, up_hbm,
    part_own, part_oth, gate_wt, up_wt, hidden_wt, high, low,
    x_s, z_s, down_s, gate_s, up_s, own_s, oth_s, wt_s, row_sems, sems, out_sems,
):
    groups, chunk, width = x_s.shape[1:]
    rows = groups * chunk

    def start(source, target, sem):
        copy = pltpu.make_async_copy(source, target, sem)
        copy.start()
        return copy

    def arrived(kind, scratch):
        return [
            start(ref.at[:, pl.ds(kind * chunk, chunk)], scratch.at[place], row_sems.at[kind, place])
            for place, ref in enumerate((own, oth))
        ]

    def halves(index, hbm, scratch):
        copies = []
        for place in range(2):
            first = pl.multiple_of(((core[0] + place) % 2) * width, width)
            source = hbm.at[:, pl.ds(first, width)] if index == 0 else hbm.at[pl.ds(first, width)]
            copies.append(start(source, scratch.at[place], sems.at[index, place]))
        return copies

    z_copies, down_copies = arrived(1, z_s), halves(0, down_hbm, down_s)
    x_copies, gate_copies = arrived(0, x_s), halves(1, gate_hbm, gate_s)
    up_copies = halves(2, up_hbm, up_s)

    def rows_of(scratch, place):
        return scratch[place].reshape(rows, width)

    def total(product, scratch, copies, weight, weight_copies):
        parts = []
        for place in range(2):
            for copy in (copies[place], weight_copies[place]):
                if copy is not None:
                    copy.wait()
            parts.append(product(rows_of(scratch, place), weight[place]))
        return parts[0] + parts[1]

    down_back = total(lin_t, z_s, z_copies, down_s, down_copies)
    gate_lin = total(lin, x_s, x_copies, gate_s, gate_copies)
    gate_sig = jax.nn.sigmoid(gate_lin)
    up_lin = total(lin, x_s, (None, None), up_s, up_copies)
    gate_act = gate_lin * gate_sig
    hidden = gate_act * up_lin
    scored = jnp.sum(hidden * down_back, axis=1, keepdims=True) * coefs[...]
    scored_b = scored.astype(BF16)
    high[...] = scored_b
    low[...] = (scored - scored_b.astype(F32)).astype(BF16)
    back = slot_w[...] * down_back
    wt_s[0] = (back * up_lin * gate_sig * (1.0 + gate_lin * (1.0 - gate_sig))).astype(BF16)
    wt_s[1] = (back * gate_act).astype(BF16)
    saves = []
    for place, router, scratch, out in ((1, router_oth, oth_s, part_oth), (0, router_own, own_s, part_own)):
        scratch[...] = (
            lin_t(wt_s[0], gate_s[place]) + lin_t(wt_s[1], up_s[place]) + lin(scored_b, router[...])
        ).astype(BF16)
        saves.append(start(scratch, out, out_sems.at[3 + place]))
        if place == 1:
            wt_s[2] = (slot_w[...] * hidden).astype(BF16)
            for k, ref in enumerate((gate_wt, up_wt, hidden_wt)):
                saves.append(start(wt_s.at[k], ref, out_sems.at[k]))
    for copy in saves:
        copy.wait()


def expert_rows(core, own, oth, slot_w, coefs, router_own, router_oth, down_w, gate_w, up_w):
    groups, span, width = own.shape
    chunk = span // 2
    rows = groups * chunk
    hidden = gate_w.shape[1]
    wide = jax.ShapeDtypeStruct((rows, width), BF16)
    deep = jax.ShapeDtypeStruct((rows, hidden), BF16)
    narrow = jax.ShapeDtypeStruct(coefs.shape, BF16)
    whole = pl.BlockSpec(memory_space=pltpu.VMEM)
    raw = pl.BlockSpec(memory_space=pl.ANY)
    return pl.pallas_call(
        expert_body,
        name="expert_rows",
        in_specs=[pl.BlockSpec(memory_space=pltpu.SMEM)] + [raw] * 2 + [whole] * 4 + [raw] * 3,
        out_specs=[raw] * 5 + [whole] * 2,
        scratch_shapes=[
            pltpu.VMEM((2, groups, chunk, width), BF16),
            pltpu.VMEM((2, groups, chunk, width), BF16),
            pltpu.VMEM((2, hidden, width), BF16),
            pltpu.VMEM((2, width, hidden), BF16),
            pltpu.VMEM((2, width, hidden), BF16),
            pltpu.VMEM((rows, width), BF16),
            pltpu.VMEM((rows, width), BF16),
            pltpu.VMEM((3, rows, hidden), BF16),
            pltpu.SemaphoreType.DMA((2, 2)),
            pltpu.SemaphoreType.DMA((3, 2)),
            pltpu.SemaphoreType.DMA((5,)),
        ],
        out_shape=[wide, wide, deep, deep, deep, narrow, narrow],
        cost_estimate=pl.CostEstimate(
            flops=20 * rows * width * hidden,
            bytes_accessed=12 * width * hidden + 12 * rows * width + 6 * rows * hidden,
            transcendentals=rows * hidden,
        ),
    )(core, own, oth, slot_w, coefs, router_own, router_oth, down_w, gate_w, up_w)


def flat(ref):
    groups, chunk, width = ref.shape
    return ref[...].reshape(groups * chunk, width)


def router_body(own_1, oth_1, own_2, oth_2, high_1, low_1, high_2, low_2, own, oth):
    for one, two, out in ((own_1, own_2, own), (oth_1, oth_2, oth)):
        x_1, x_2 = flat(one), flat(two)
        out[...] = (
            lin_rows(high_1[...], x_1) + lin_rows(low_1[...], x_1)
            + lin_rows(high_2[...], x_2) + lin_rows(low_2[...], x_2)
        )


def router_grads(own_1, oth_1, own_2, oth_2, *scores):
    groups, _, width = own_1.shape
    experts = scores[0].shape[1]
    rows = scores[0].shape[0] + scores[2].shape[0]
    tile = FEATURE_TILE if width % FEATURE_TILE == 0 else width
    out = jax.ShapeDtypeStruct((experts, width), F32)
    blocks = [
        pl.BlockSpec((groups, ref.shape[1] // 2, tile), lambda i: (0, 0, i))
        for ref in (own_1, oth_1, own_2, oth_2)
    ]
    full = [pl.BlockSpec(score.shape, lambda i: (0, 0)) for score in scores]
    return pl.pallas_call(
        router_body,
        name="router_grads",
        grid=(width // tile,),
        in_specs=blocks + full,
        out_specs=[pl.BlockSpec((experts, tile), lambda i: (0, i))] * 2,
        out_shape=[out, out],
        cost_estimate=pl.CostEstimate(
            flops=8 * rows * width * experts,
            bytes_accessed=4 * rows * width,
            transcendentals=0,
        ),
    )(own_1, oth_1, own_2, oth_2, *scores)


def weight_body(
    core, x_1, z_1, x_2, z_2, gate_1, up_1, hidden_1, gate_2, up_2, hidden_2, *refs
):
    grad_gate, grad_up, grad_down = refs[-3:]
    first, second = flat(x_1), flat(x_2)
    grad_gate[...] = (lin_rows(first, gate_1[...]) + lin_rows(second, gate_2[...])).astype(BF16)
    grad_up[...] = (lin_rows(first, up_1[...]) + lin_rows(second, up_2[...])).astype(BF16)
    grad_down[...] = (
        lin_rows(hidden_1[...], flat(z_1)) + lin_rows(hidden_2[...], flat(z_2))
    ).astype(BF16)


def weight_grads(core, place, part_1, part_2, weighted, begun=()):
    groups, _, width = part_1.shape
    hidden = weighted[0].shape[1]
    rows = weighted[0].shape[0] + weighted[3].shape[0]
    tile = FEATURE_TILE if width % FEATURE_TILE == 0 else width
    steps = width // tile

    def block(ref, kind):
        return pl.BlockSpec(
            (groups, ref.shape[1] // 2, tile), lambda i, core: (0, kind, i)
        )

    blocks = [block(ref, kind) for ref in (part_1, part_2) for kind in range(2)]
    full = [pl.BlockSpec(value.shape, lambda i, core: (0, 0)) for value in weighted]
    raw = [pl.BlockSpec(memory_space=pl.ANY)] * len(begun)
    by_rows = pl.BlockSpec((tile, hidden), lambda i, core: (((core[0] + place) % 2) * steps + i, 0))
    by_columns = pl.BlockSpec((hidden, tile), lambda i, core: (0, ((core[0] + place) % 2) * steps + i))
    tall = jax.ShapeDtypeStruct((2 * width, hidden), BF16)
    return pl.pallas_call(
        weight_body,
        name="weight_grads",
        grid_spec=pltpu.PrefetchScalarGridSpec(
            num_scalar_prefetch=1,
            grid=(steps,),
            in_specs=blocks + full + raw,
            out_specs=[by_rows, by_rows, by_columns],
        ),
        out_shape=[tall, tall, jax.ShapeDtypeStruct((hidden, 2 * width), BF16)],
        input_output_aliases={11 + k: k for k in range(len(begun))},
        cost_estimate=pl.CostEstimate(
            flops=6 * rows * width * hidden,
            bytes_accessed=6 * width * hidden + 4 * rows * width + 6 * rows * hidden,
            transcendentals=0,
        ),
    )(core, part_1, part_1, part_2, part_2, *weighted, *begun)


FILL_BYTES = 24 * 2**20


def fill_body(first, targets, x_rows, z_rows, out):
    experts, span, width = out.shape
    chunk = span // 2
    capacity = 3 * targets.shape[1] // experts
    rows = experts * chunk
    index = lax.broadcasted_iota(jnp.int32, (rows, targets.shape[1]), 0)
    ids = (index // chunk * capacity + index % chunk + first).astype(F32)
    hit = (targets[0:1, :] == ids) | (targets[1:2, :] == ids)
    fill = jnp.where(hit, 1.0, 0.0).astype(BF16)
    out[:, :chunk, :] = lin(fill, x_rows[...]).astype(BF16).reshape(experts, chunk, width)
    out[:, chunk:, :] = lin(fill, z_rows[...]).astype(BF16).reshape(experts, chunk, width)


def fill_slots(targets, x_rows, z_rows, experts, first, chunk):
    width = x_rows.shape[1]
    return pl.pallas_call(
        functools.partial(fill_body, first),
        name="fill_slots",
        compiler_params=pltpu.CompilerParams(vmem_limit_bytes=FILL_BYTES),
        out_shape=jax.ShapeDtypeStruct((experts, 2 * chunk, width), BF16),
    )(targets, x_rows, z_rows)


def token_body(
    routes, own_sums, oth_sums, latents, cotangent, shift, scale, gate,
    out, normed_b, scaled_dy, targets,
):
    experts, span, width = out.shape
    chunk = span // 2
    tokens = routes.shape[1]
    capacity = 3 * tokens // experts
    expert_ids = lax.broadcasted_iota(jnp.int32, (experts, tokens), 0)
    named = [jnp.where(routes[k:k + 1, :] == expert_ids, 1.0, 0.0) for k in range(2)]
    rows_i = lax.broadcasted_iota(jnp.int32, (tokens, tokens), 0)
    cols_i = lax.broadcasted_iota(jnp.int32, (tokens, tokens), 1)
    earlier = jnp.where(rows_i < cols_i, 1.0, 0.0).astype(BF16)
    places = lin((named[0] + named[1]).astype(BF16), earlier)
    places = places + (expert_ids * capacity).astype(F32)
    for k in range(2):
        targets[k:k + 1, :] = jnp.sum(named[k] * places, axis=0, keepdims=True)
    sums = (own_sums[...] + oth_sums[...]) / (2 * width)
    inv_std = lax.rsqrt(sums[1:2] - sums[0:1] * sums[0:1] + norm_eps)

    def column(row):
        return jnp.broadcast_to(row, (8, tokens)).T[:, 0:1]

    normed = (latents[...].astype(F32) - column(sums[0:1])) * column(inv_std)
    normed = normed * (1.0 + scale[...].astype(F32)) + shift[...].astype(F32)
    x_rows = normed.astype(BF16)
    z_rows = (gate[...].astype(F32) * cotangent[...].astype(F32)).astype(BF16)
    normed_b[...] = x_rows
    scaled_dy[...] = z_rows
    index = lax.broadcasted_iota(jnp.int32, (experts * chunk, tokens), 0)
    ids = (index // chunk * capacity + index % chunk).astype(F32)
    hit = (targets[0:1, :] == ids) | (targets[1:2, :] == ids)
    fill = jnp.where(hit, 1.0, 0.0).astype(BF16)
    out[:, :chunk, :] = lin(fill, x_rows).astype(BF16).reshape(experts, chunk, width)
    out[:, chunk:, :] = lin(fill, z_rows).astype(BF16).reshape(experts, chunk, width)


def token_slots(routes, own_sums, oth_sums, latents, cotangent, shift, scale, gate, experts, chunk):
    tokens, width = latents.shape
    rows = jax.ShapeDtypeStruct((tokens, width), BF16)
    return pl.pallas_call(
        token_body,
        name="token_slots",
        out_shape=[
            jax.ShapeDtypeStruct((experts, 2 * chunk, width), BF16), rows, rows,
            jax.ShapeDtypeStruct(routes.shape, F32),
        ],
    )(routes, own_sums, oth_sums, latents, cotangent, shift, scale, gate)


def per_device(
    latents, cotangent, routes, router_w, mod_shift, mod_scale, mod_gate, gate_w, up_w, down_w
):
    size = lax.axis_size("dp")
    if lax.axis_size("expert") != 2 or size & (size - 1) or gate_w.shape[0] != 1 or latents.shape[0] % 256:
        return spread_device(
            latents, cotangent, routes, router_w, mod_shift, mod_scale, mod_gate,
            gate_w, up_w, down_w,
        )
    tok_rows, width = latents.shape
    experts = router_w.shape[1]
    entire_width = 2 * width
    capacity = 3 * tok_rows // experts
    slot_count = experts * capacity
    dp_index = lax.axis_index("dp")
    sample_index = dp_index * tok_rows // SEQ
    core = lax.axis_index("expert").astype(jnp.int32).reshape(1)
    gate_w, up_w, down_w = gate_w[0], up_w[0], down_w[0]

    first = capacity // 3 * 2
    parts = ((0, first), (first, capacity - first))

    def slot_of(index, first, length):
        return (index // length * capacity + index % length + first).astype(F32)

    def mod_row(table):
        return lax.dynamic_slice_in_dim(table, sample_index, 1, 0)

    x = latents.astype(F32)
    own_sums = jnp.stack([jnp.sum(x, axis=1), jnp.sum(x * x, axis=1)])
    oth_sums = pair_swap(own_sums)
    second = capacity - first
    send_1, normed_b, scaled_dy, targets = token_slots(
        routes.T, own_sums, oth_sums, latents, cotangent,
        mod_row(mod_shift), mod_row(mod_scale), mod_row(mod_gate), experts, first,
    )
    own_sums, latents, mod_shift, mod_scale, routes, _ = lax.optimization_barrier(
        (own_sums, latents, mod_shift, mod_scale, routes, send_1)
    )
    expert_ids = lax.broadcasted_iota(jnp.int32, (experts, tok_rows), 0)
    named = [routes[:, k][None, :] == expert_ids for k in range(2)]
    cot = cotangent.astype(F32)
    x = latents.astype(F32)
    mean, msq = (own_sums + oth_sums) / entire_width
    inv_std = lax.rsqrt(msq - mean * mean + norm_eps)[:, None]
    xhat = (x - mean[:, None]) * inv_std
    amp = 1.0 + selected_row(mod_scale, sample_index)
    normed = xhat * amp + selected_row(mod_shift, sample_index)
    send_2 = fill_slots(
        targets, normed_b, scaled_dy, experts, first, second
    )
    own_1 = all_to_all(send_1)
    own_2 = all_to_all(send_2)

    logits = core_sum(lax.dot_general(
        router_w, after(normed, send_1), (((0,), (1,)), ((), ())), precision=HIGHEST
    ))
    chances = jax.nn.sigmoid(logits)
    picked = jnp.stack([jnp.sum(jnp.where(n, chances, 0.0), axis=0) for n in named])
    pick_sum = jnp.sum(picked, axis=0, keepdims=True)
    weights = picked / pick_sum
    slopes = weights[::-1] * picked * (1.0 - picked) / pick_sum
    other_ids = routes.T[::-1].astype(F32)
    slot_row = lax.broadcasted_iota(jnp.int32, (tok_rows, slot_count), 1).astype(F32)
    hits = [t[:, None] == slot_row for t in targets]

    def of_slots(pair):
        return jnp.sum(
            jnp.where(hits[0], pair[0][:, None], 0.0) + jnp.where(hits[1], pair[1][:, None], 0.0),
            axis=0,
        ).reshape(experts, capacity)

    kinds = (weights, slopes, slopes[::-1], other_ids)
    sent = jnp.concatenate([of_slots(pair) for pair in kinds], axis=1)
    arrived = dp_exchange(sent)
    columns = []
    for start, length in parts:
        rows = experts * length
        ids = lax.broadcasted_iota(jnp.int32, (rows, experts), 1).astype(F32)
        slot_w, slope, slope_other, other = [
            arrived[:, k * capacity + start:k * capacity + start + length].reshape(rows, 1)
            for k in range(4)
        ]
        coefs = jnp.where(ids == dp_index.astype(F32), slope, 0.0) - jnp.where(
            ids == other, slope_other, 0.0
        )
        columns.append((slot_w, coefs))
    router_own = router_w.T.astype(BF16)
    router_oth = pair_swap(after(router_own, send_1))
    joins = []
    for start, length in parts:
        ids = slot_of(
            lax.broadcasted_iota(jnp.int32, (tok_rows, experts * length), 1), start, length
        )
        joins.append(((targets[0][:, None] == ids) | (targets[1][:, None] == ids)).astype(BF16))

    oth_1 = pair_swap(own_1)
    part_own, part_oth, gate_1, up_1, hidden_1, high_1, low_1 = expert_rows(
        core, own_1, oth_1, *columns[0], router_own, router_oth, down_w, gate_w, up_w
    )
    back_1 = (part_own.astype(F32) + pair_swap(part_oth).astype(F32)).astype(BF16)
    back_1 = all_to_all(after(back_1, own_2).reshape(experts, first, width))
    oth_2 = pair_swap(own_2)
    part_own, part_oth, gate_2, up_2, hidden_2, high_2, low_2 = expert_rows(
        core, own_2, oth_2, *columns[1], router_own, router_oth, down_w, gate_w, up_w
    )
    back_2 = (part_own.astype(F32) + pair_swap(part_oth).astype(F32)).astype(BF16)
    weighted = (gate_1, up_1, hidden_1, gate_2, up_2, hidden_2)
    begun = weight_grads(core, 0, after(own_1, back_2), own_2, weighted)
    back_2 = all_to_all(after(back_2, back_1).reshape(experts, second, width))

    router_own, router_oth = router_grads(own_1, oth_1, own_2, oth_2, high_1, low_1, high_2, low_2)
    grad_gate, grad_up, grad_down = weight_grads(
        core, 1, oth_1, oth_2, weighted, begun
    )
    grad_router = dp_total(router_own + pair_swap(router_oth)).T

    combined = lin(joins[0], back_1.reshape(-1, width))
    dxhat = (combined + lin(joins[1], back_2.reshape(-1, width))) * amp
    m_one, m_two = core_sum(
        jnp.stack([jnp.sum(dxhat, axis=1), jnp.sum(dxhat * xhat, axis=1)])
    ) / entire_width
    latent_gradient = inv_std * (dxhat - m_one[:, None] - xhat * m_two[:, None]) + cot
    return (
        latent_gradient.astype(BF16), grad_gate[None], grad_up[None], grad_down[None], grad_router
    )


def solution(mesh):
    placed = (
        P("dp", "expert"),
        P("dp", "expert"),
        P("dp", None),
        P("expert", None),
        P(None, "expert"),
        P(None, "expert"),
        P(None, "expert"),
        P("dp", None, "expert"),
        P("dp", None, "expert"),
        P("dp", "expert", None),
    )
    return jax.shard_map(
        per_device,
        mesh=mesh,
        in_specs=placed,
        out_specs=(
            P("dp", "expert"),
            P("dp", None, "expert"),
            P("dp", None, "expert"),
            P("dp", "expert", None),
            P("expert", None),
        ),
        check_vma=False,
    )
```
